256 devices in a mesh: section: 16 (over x, y), tensor: 16 (over z, core).
Axes of the slice: x: 4, y: 4, z: 8, core: 2. Of those that a mesh axis runs over, the one named last changes fastest.
Arguments:
- queries: bfloat16 [16, 512, 8192], P('section', None, 'tensor'), may hold values from -20 to 20
- key_rows: bfloat16 [16, 512, 1024], P('section'), may hold values from -6 to 6
- value_rows: bfloat16 [16, 512, 1024], P('section'), may hold values from -6 to 6
- out_grad: bfloat16 [16, 512, 8192], P('section', None, 'tensor'), may hold values from -24 to 24
- layer_input: bfloat16 [16, 512, 8192], P('section', 'tensor'), may hold values from -64 to 64
- query_weight: bfloat16 [16, 8192, 8192], P('section', None, 'tensor'), may hold values from -0.0625 to 0.0625
- dion_basis: float32 [16, 8192, 256], P('section', 'tensor'), may hold values from -0.0625 to 0.0625
- lengths: int32 [16, 3], P('section'), may hold values from 1 to 256, 512 in all within a row
Outputs:
- upstream: bfloat16 [16, 512, 8192], P('section', 'tensor')
- left_factor: float32 [16, 8192, 256], P('section', 'tensor')
- right_factor: float32 [16, 8192, 256], P('section', 'tensor')
The draws below stay inside these ranges and needn't reach their ends.
Inputs may be any that keep to these rules, and one draw needn't show every extreme that they name: For each section the lengths of the prompt, the chosen and the rejected response, in that order, summing to 512.
All inputs are finite; a program needn't handle non-finite values.
Results may differ from the reference program's by a relative error of at most 0.022.
Values may be sent and summed in bfloat16 or wider, within the bound.
No kernel may reach another device: no remote copies, remote signals or barrier semaphores. Data moves between devices by JAX's collectives and lax.ppermute only.
A program may use at most 64 MiB of HBM per device.

```python
import math
import jax
import jax.numpy as jnp
import numpy as np
from jax import lax

D = 8192
HEADS = 64
HD = 128
GROUP = 8
KV_HEADS = 8
TOK = 512
RANK = 256
N_SECTION = 16
N_TENSOR = 16


def paired_draw(key):
    query_key = jax.random.fold_in(key, 101)
    key_key = jax.random.fold_in(key, 202)
    queries = jnp.clip(jax.random.normal(query_key, (N_SECTION, TOK, HEADS * HD), jnp.float32), -6.0, 6.0)
    key_rows = jnp.clip(jax.random.normal(key_key, (N_SECTION, TOK, HEADS // GROUP * HD), jnp.float32), -6.0, 6.0)
    return (queries, key_rows)


def draw_queries(key, part):
    return paired_draw(key)[0].astype(jnp.bfloat16)


def draw_key_rows(key, part):
    return paired_draw(key)[1].astype(jnp.bfloat16)


def draw_layer_input(key, part):
    base_key = jax.random.fold_in(key, 404)
    column_key = jax.random.fold_in(key, 505)
    row_key = jax.random.fold_in(key, 606)
    column_ids = jnp.arange(D, dtype=jnp.float32)
    ramp = jnp.power(10.0, column_ids / (D - 1.0) - 0.5)
    rough = jax.random.uniform(column_key, (N_SECTION, 1, D), jnp.float32, 0.7, 1.3)
    row_scale = jax.random.uniform(row_key, (N_SECTION, TOK, 1), jnp.float32, 0.6, 1.6)
    base = jnp.clip(jax.random.normal(base_key, (N_SECTION, TOK, D), jnp.float32), -6.0, 6.0)
    return (base * ramp[None, None, :] * rough * row_scale).astype(jnp.bfloat16)


def steps_of(rng, dims, split, smallest, top_value):
    factor_of, own = 1.0, jax.random.fold_in(rng, 6)
    for dim, shards_of in split:
        heights = jnp.exp(jax.random.uniform(jax.random.fold_in(own, dim), (shards_of,), jnp.float32, smallest / len(split), top_value / len(split)))
        factor_of = factor_of * jnp.repeat(heights, dims[dim] // shards_of).reshape([-1 if axis == dim else 1 for axis in range(len(dims))])
    return factor_of


def split_up(count, total, reach, slope):
    loads = [(1 << 20) // math.isqrt(standing ** slope) + 1 for standing in range(2, count + 1)]
    spare, counts = total - reach - (count - 1), [1] * (count - 1)
    while spare > 0:
        movable = [i for i in range(count - 1) if counts[i] < reach]
        mass, left = sum([loads[i] for i in movable]), spare
        for i in movable:
            extra = min(reach - counts[i], max(1, left * loads[i] // mass), spare)
            counts[i] = counts[i] + extra
            spare = spare - extra
    return np.array([reach] + counts)


def uneven_parts(own_key, count, total, reach, slope):
    if count == 2:
        one = jax.random.randint(own_key, (), max(1, total - reach), min(reach, total - 1) + 1)
        return jnp.stack([one, total - one])
    sizes = jnp.asarray(split_up(count, total, reach, slope), jnp.int32)
    twos = (count - 1) // 2
    giver, receiver = sizes[1:1 + 2 * twos:2], sizes[2:2 + 2 * twos:2]
    room = jnp.minimum(giver - 1, reach - receiver)
    moved = jax.random.randint(jax.random.fold_in(own_key, 1), (twos,), 0, 1 << 20) % (room + 1)
    sizes = sizes.at[1:1 + 2 * twos:2].set(giver - moved).at[2:2 + 2 * twos:2].set(receiver + moved)
    return sizes[jax.random.permutation(jax.random.fold_in(own_key, 2), count)]


def noise(stream_key, extent, scale, most, pieces=(), kind=jnp.bfloat16):
    array = jax.random.normal(stream_key, extent, jnp.float32) * scale
    if len(pieces) > 0:
        array = steps_of(stream_key, extent, pieces, -0.22, 0.18) * array
    return jnp.clip(array, min=-most, max=most).astype(kind)


def setup_inputs(seed: int = 0) -> dict:
    key_of = jax.random.split(jax.random.key(seed), 9)
    queries = draw_queries(jax.random.fold_in(key_of[8], 71), 0)
    key_rows = draw_key_rows(jax.random.fold_in(key_of[8], 71), 0)
    value_rows = noise(key_of[2], (N_SECTION, TOK, KV_HEADS * HD), 1.0, 6.0, ((0, 16),))
    out_grad = noise(key_of[3], (N_SECTION, TOK, HEADS * HD), 4.0, 24.0, ((0, 16), (2, 16)))
    layer_input = draw_layer_input(jax.random.fold_in(key_of[8], 71), 0)
    query_weight = noise(key_of[5], (N_SECTION, D, HEADS * HD), D ** -0.5, 0.0625, ((0, 16), (2, 16)))
    dion_basis = noise(key_of[6], (N_SECTION, HEADS * HD, RANK), (HEADS * HD) ** -0.5, 0.0625, ((0, 16), (1, 16)), jnp.float32)
    lengths = jax.vmap(lambda own: uneven_parts(own, 3, TOK, TOK // 2, 1))(jax.random.split(key_of[7], N_SECTION)).reshape((N_SECTION, 3)).astype(jnp.int32)
    return dict(queries=queries, key_rows=key_rows, value_rows=value_rows, out_grad=out_grad, layer_input=layer_input, query_weight=query_weight, dion_basis=dion_basis, lengths=lengths)


rope_base = 500000.0
highest = lax.Precision.HIGHEST

def tree_layout(lengths_row, token_count):
    token_ids = jnp.arange(token_count, dtype=jnp.int32)
    bound_one = lengths_row[0]
    bound_two = lengths_row[0] + lengths_row[1]
    positions = jnp.where(token_ids < bound_two, token_ids, token_ids - lengths_row[1]).astype(jnp.float32)
    row_ids = token_ids[:, None]
    col_ids = token_ids[None, :]
    crossed = (row_ids >= bound_two) & (col_ids >= bound_one) & (col_ids < bound_two)
    visible = (col_ids <= row_ids) & jnp.logical_not(crossed)
    return (positions, visible)

def unrotate(rotated, positions):
    head_dim = rotated.shape[-1]
    half_dim = head_dim // 2
    freq_ids = jnp.arange(half_dim, dtype=jnp.float32)
    inverse = jnp.exp(-math.log(rope_base) * 2.0 * freq_ids / head_dim)
    angles = positions[:, None] * inverse[None, :]
    cosine = jnp.cos(angles)[:, None, :]
    sine_part = jnp.sin(angles)[:, None, :]
    first_half = rotated[..., :half_dim]
    second_half = rotated[..., half_dim:]
    return jnp.concatenate([first_half * cosine + second_half * sine_part, second_half * cosine - first_half * sine_part], axis=-1)

def group_backward(query_block, grad_block, key_block, value_block, visible):
    score_scale = 1.0 / math.sqrt(query_block.shape[-1])
    query_wide = query_block.astype(jnp.float32)
    grad_wide = grad_block.astype(jnp.float32)
    key_wide = key_block.astype(jnp.float32)
    value_wide = value_block.astype(jnp.float32)
    scores = jnp.einsum('qhd,kd->hqk', query_wide, key_wide) * score_scale
    scores = jnp.where(visible[None], scores, -jnp.inf)
    row_max = lax.optimization_barrier(jnp.max(scores, axis=-1, keepdims=True))
    exp_scores = jnp.exp(scores - row_max)
    weights = exp_scores / lax.optimization_barrier(jnp.sum(exp_scores, axis=-1, keepdims=True))
    weights_low = weights.astype(jnp.bfloat16)
    outputs = jnp.einsum('hqk,kd->qhd', weights_low.astype(jnp.float32), value_wide)
    out_dot = lax.optimization_barrier(jnp.sum(grad_wide * outputs, axis=-1))
    prob_grad = jnp.einsum('qhd,kd->hqk', grad_wide, value_wide)
    score_grad = (weights * (prob_grad - out_dot.T[:, :, None])).astype(jnp.bfloat16)
    return jnp.einsum('hqk,kd->qhd', score_grad.astype(jnp.float32), key_wide) * score_scale

def section_backward(section_items):
    queries, key_rows, value_rows, out_grad, layer_input, query_weight, dion_basis, lengths = section_items
    token_count = queries.shape[0]
    positions, visible = tree_layout(lengths, token_count)
    query_heads = queries.reshape(token_count, HEADS, HD)
    grad_heads = out_grad.reshape(token_count, HEADS, HD)

    def one_group(group_id):
        query_block = lax.dynamic_slice_in_dim(query_heads, (group_id * GROUP).astype(jnp.int32), GROUP, 1)
        grad_block = lax.dynamic_slice_in_dim(grad_heads, (group_id * GROUP).astype(jnp.int32), GROUP, 1)
        key_block = lax.dynamic_slice_in_dim(key_rows, (group_id * HD).astype(jnp.int32), HD, 1)
        value_block = lax.dynamic_slice_in_dim(value_rows, (group_id * HD).astype(jnp.int32), HD, 1)
        return group_backward(query_block, grad_block, key_block, value_block, visible)
    rotated = lax.map(one_group, jnp.arange(HEADS // GROUP, dtype=jnp.int32))
    rotated = jnp.transpose(rotated, (1, 0, 2, 3)).reshape(token_count, HEADS, HD)
    query_grad = unrotate(rotated, positions).reshape(token_count, HEADS * HD).astype(jnp.bfloat16)
    block_width = HEADS * HD // N_TENSOR

    def add_block(block_id, running):
        block_start = jnp.asarray(block_id * block_width).astype(jnp.int32)
        grad_piece = lax.dynamic_slice_in_dim(query_grad, block_start, block_width, 1)
        weight_piece = lax.dynamic_slice_in_dim(query_weight, block_start, block_width, 1)
        partial_sum = lax.dot_general(grad_piece.astype(jnp.float32), weight_piece.astype(jnp.float32), (((1,), (1,)), ((), ())), preferred_element_type=jnp.float32)
        rounded = lax.optimization_barrier(partial_sum.astype(jnp.bfloat16))
        return running + rounded.astype(jnp.float32)
    layer_grad = lax.fori_loop(0, N_TENSOR, add_block, jnp.zeros((token_count, D), jnp.float32)).astype(jnp.bfloat16)
    grad_wide = query_grad.astype(jnp.float32)
    input_wide = layer_input.astype(jnp.float32)
    projected = jnp.dot(grad_wide, dion_basis, precision=highest)
    left_raw = lax.dot_general(input_wide, projected, (((0,), (0,)), ((), ())), precision=highest)
    gram_total = lax.dot_general(left_raw, left_raw, (((0,), (0,)), ((), ())), precision=highest)
    lower_factor = jnp.linalg.cholesky(gram_total)
    left_orth = lax.linalg.triangular_solve(lower_factor, left_raw, left_side=False, lower=True, transpose_a=True)
    mixed = jnp.dot(input_wide, left_orth, precision=highest)
    right_factor = lax.dot_general(grad_wide, mixed, (((0,), (0,)), ((), ())), precision=highest)
    return (layer_grad, left_orth * math.sqrt(D), right_factor)

def reference(queries, key_rows, value_rows, out_grad, layer_input, query_weight, dion_basis, lengths):
    layer_grad, left_factor, right_factor = lax.map(section_backward, (queries, key_rows, value_rows, out_grad, layer_input, query_weight, dion_basis, lengths))
    upstream = jnp.concatenate([layer_grad[1:], jnp.zeros_like(layer_grad[:1])], axis=0)
    return (upstream, left_factor, right_factor)
```

```python
import functools
import math

import jax
import jax.numpy as jnp
from jax import lax
from jax.experimental import pallas as pl
from jax.experimental.pallas import tpu as pltpu
from jax.sharding import PartitionSpec as P

D = 8192
HD = 128
GROUP = 8
ZN = 8
CHUNK = 32

rope_base = 500000.0
highest = lax.Precision.HIGHEST
z_groups = [[2 * z + core for z in range(ZN)] for core in range(2)]


def dot_f32(a, b, dims, precision=None):
    return lax.dot_general(a, b, (dims, ((), ())), precision=precision, preferred_element_type=jnp.float32)


def attention_kernel(info, lens, cos_ref, sin_ref, q_ref, g_ref, k_ref, v_ref, out_ref):
    block = 128
    tokens = q_ref.shape[1]
    scale = 1.0 / math.sqrt(HD)
    bound_one = lens[0, 0]
    bound_two = lens[0, 0] + lens[0, 1]
    for row in range(0, tokens, block):
        keys = row + block
        q = q_ref[0, row : row + block, :]
        g = g_ref[0, row : row + block, :]
        k = k_ref[0, :keys, :]
        v = v_ref[0, :keys, :]
        s = dot_f32(q, k, ((1,), (1,))) * scale
        i = row + lax.broadcasted_iota(jnp.int32, s.shape, 0)
        j = lax.broadcasted_iota(jnp.int32, s.shape, 1)
        crossed = (i >= bound_two) & (j >= bound_one) & (j < bound_two)
        visible = (j <= i) & jnp.logical_not(crossed)
        s = jnp.where(visible, s, -jnp.inf)
        e = jnp.exp(s - jnp.max(s, axis=-1, keepdims=True))
        w = e * (1.0 / jnp.sum(e, axis=-1, keepdims=True))
        o = dot_f32(w.astype(jnp.bfloat16), v, ((1,), (0,)))
        out_dot = jnp.sum(g.astype(jnp.float32) * o, axis=-1, keepdims=True)
        dp = dot_f32(g, v, ((1,), (1,)))
        ds = (w * (dp - out_dot)).astype(jnp.bfloat16)
        r = dot_f32(ds, k, ((1,), (0,))) * scale
        turned = jnp.concatenate([r[:, HD // 2 :], r[:, : HD // 2]], axis=1)
        r = r * cos_ref[row : row + block, :] + turned * sin_ref[row : row + block, :]
        out_ref[row : row + block, :] = r.astype(jnp.bfloat16)


def attention(info, lengths, cosine, sine, queries, out_grad, key_rows, value_rows):
    tokens, width = queries.shape[1:]
    heads = width // HD
    head_block = pl.BlockSpec((1, tokens, HD), lambda h, info, lens: (0, 0, h))
    kv_block = pl.BlockSpec((1, tokens, HD), lambda h, info, lens: (0, 0, info[2]))
    whole = pl.BlockSpec((tokens, HD), lambda h, info, lens: (0, 0))
    return pl.pallas_call(
        attention_kernel,
        out_shape=jax.ShapeDtypeStruct((tokens, width), jnp.bfloat16),
        grid_spec=pltpu.PrefetchScalarGridSpec(
            num_scalar_prefetch=2,
            grid=(heads,),
            in_specs=[whole, whole, head_block, head_block, kv_block, kv_block],
            out_specs=pl.BlockSpec((tokens, HD), lambda h, info, lens: (0, h)),
        ),
        compiler_params=pltpu.CompilerParams(vmem_limit_bytes=40 << 20),
        cost_estimate=pl.CostEstimate(
            flops=heads * 5 * 2 * tokens * tokens * HD, bytes_accessed=4 << 20, transcendentals=heads * tokens * tokens
        ),
        name="attention_backward",
    )(info, lengths, cosine, sine, queries, out_grad, key_rows, value_rows)


def layer_kernel(info, mine_ref, other_ref, w_mine_ref, w_other_ref, out_ref, rows_a, rows_b):
    z, core = info[0], info[1]

    @pl.when(pl.program_id(0) == 0)
    def _():
        for r in range(ZN):
            chip = lax.rem(z + r, ZN) * (2 * CHUNK)
            for half in range(2):
                start = pl.multiple_of(chip + (core ^ half) * CHUNK, CHUNK)
                target = slice((2 * r + half) * CHUNK, (2 * r + half + 1) * CHUNK)
                rows_a[target, :] = mine_ref[pl.ds(start, CHUNK), :]
                rows_b[target, :] = other_ref[pl.ds(start, CHUNK), :]

    total = dot_f32(rows_a[...], w_mine_ref[0], ((1,), (1,)))
    total += dot_f32(rows_b[...], w_other_ref[...], ((1,), (1,)))
    out_ref[...] = total.astype(jnp.bfloat16)


def layer_partial(info, mine, other, w_mine, w_other):
    tokens, width = mine.shape
    half = w_other.shape[0]
    tile = 512
    steps = half // tile
    whole = pl.BlockSpec((tokens, width), lambda i, info: (0, 0))
    return pl.pallas_call(
        layer_kernel,
        out_shape=jax.ShapeDtypeStruct((tokens, half), jnp.bfloat16),
        grid_spec=pltpu.PrefetchScalarGridSpec(
            num_scalar_prefetch=1,
            grid=(steps,),
            in_specs=[
                whole,
                whole,
                pl.BlockSpec((1, tile, width), lambda i, info: (0, info[1] * steps + i, 0)),
                pl.BlockSpec((tile, width), lambda i, info: (i, 0)),
            ],
            out_specs=pl.BlockSpec((tokens, tile), lambda i, info: (0, i)),
            scratch_shapes=[pltpu.VMEM((tokens, width), jnp.bfloat16)] * 2,
        ),
        compiler_params=pltpu.CompilerParams(vmem_limit_bytes=40 << 20),
        cost_estimate=pl.CostEstimate(flops=4 * tokens * width * half, bytes_accessed=13 << 20, transcendentals=0),
        name="layer_partial",
    )(info, mine, other, w_mine, w_other)


def split_three(value):
    high = value.astype(jnp.bfloat16)
    rest = value - high.astype(jnp.float32)
    middle = rest.astype(jnp.bfloat16)
    low = (rest - middle.astype(jnp.float32)).astype(jnp.bfloat16)
    return high, middle, low


def times_exact(narrow, wide):
    parts = [dot_f32(narrow, part, ((0,), (0,))) for part in split_three(wide)]
    return parts[0] + (parts[1] + parts[2])


def dion_kernel(info, p_ref, m_ref, x_ref, g_ref, left_ref, right_ref, work):
    rank = p_ref.shape[1]
    b = 64
    p = p_ref[...]
    m = m_ref[...]
    work[:, :rank] = dot_f32(p, m, ((0,), (0,)), highest)
    rows = lax.broadcasted_iota(jnp.int32, (rank, rank), 0)
    cols = lax.broadcasted_iota(jnp.int32, (rank, rank), 1)
    work[:, rank:] = (rows == cols).astype(jnp.float32)
    rows_b = lax.broadcasted_iota(jnp.int32, (b, b), 0)
    cols_b = lax.broadcasted_iota(jnp.int32, (b, b), 1)
    eye = rows_b == cols_b
    sub = lax.broadcasted_iota(jnp.int32, (8, 1), 0)
    for block in range(0, rank, b):
        here = slice(block, block + b)
        both = jnp.concatenate([work[here, block : block + b], eye.astype(jnp.float32)], axis=1)
        groups = [both[8 * n : 8 * n + 8, :] for n in range(b // 8)]
        pivots = []
        for j in range(b):
            own = j // 8
            line = groups[own][j % 8 : j % 8 + 1, :]
            pivot = line[:, j : j + 1]
            pivots.append(pivot)
            scaled = line * (1.0 / pivot)
            for n in range(own, b // 8):
                factor = groups[n][:, j : j + 1]
                if n == own:
                    factor = jnp.where(sub > j % 8, factor, 0.0)
                groups[n] = groups[n] - factor * scaled
        done = jnp.concatenate(groups, axis=0)
        diagonal = jnp.concatenate(pivots, axis=0)
        inverse = done[:, b:] * (1.0 / jnp.sqrt(diagonal))
        strip = dot_f32(inverse, work[here, :], ((1,), (0,)), highest)
        work[here, :] = strip
        if block + b < rank:
            below = strip[:, block + b : rank]
            work[block + b :, :] -= dot_f32(below, strip, ((0,), (0,)), highest)
    lower_inverse = work[:, rank:]
    left_mix = dot_f32(p, lower_inverse, ((1,), (1,)), highest) * math.sqrt(D)
    left_ref[0] = times_exact(x_ref[...], left_mix)
    right_mix = dot_f32(m, lower_inverse, ((1,), (1,)), highest)
    right_ref[0] = times_exact(g_ref[...], right_mix)


def dion_factors(info, projected, mixed, inputs, query_grad):
    tokens, rank = projected.shape
    width = query_grad.shape[1]
    whole = pl.BlockSpec((tokens, rank), lambda i, info: (0, 0))
    result = pl.BlockSpec((1, width, rank), lambda i, info: (0, 0, 0))
    return pl.pallas_call(
        dion_kernel,
        out_shape=[jax.ShapeDtypeStruct((1, width, rank), jnp.float32)] * 2,
        grid_spec=pltpu.PrefetchScalarGridSpec(
            num_scalar_prefetch=1,
            grid=(1,),
            in_specs=[
                whole,
                whole,
                pl.BlockSpec((tokens, width), lambda i, info: (0, info[1])),
                pl.BlockSpec((tokens, width), lambda i, info: (0, 0)),
            ],
            out_specs=[result, result],
            scratch_shapes=[pltpu.VMEM((rank, 2 * rank), jnp.float32)],
        ),
        compiler_params=pltpu.CompilerParams(vmem_limit_bytes=40 << 20),
        cost_estimate=pl.CostEstimate(flops=12 << 30, bytes_accessed=4 << 20, transcendentals=0),
        name="dion_factors",
    )(info, projected, mixed, inputs, query_grad)


def swap_cores(value):
    return lax.ppermute(value, "tensor", [(i, i ^ 1) for i in range(2 * ZN)])


def along_z(value, steps):
    count = 2 * ZN
    return lax.ppermute(value, "tensor", [(i, (i + 2 * steps) % count) for i in range(count)])


def exchange_z(value):
    return lax.all_to_all(value, "tensor", 0, 0, tiled=True, axis_index_groups=z_groups)


def tree_reduce_scatter(parts):
    half = parts[0].shape[1] // 2
    a = [part[:, :half] for part in parts]
    b = [part[:, half:] for part in parts]
    a_up, a_down = a[4], a[5]
    b_up, b_down = b[3], b[4]
    for k in range(4):
        a_up = along_z(a_up, 1)
        b_down = along_z(b_down, -1)
        if k < 3:
            a_up = a_up + a[3 - k]
            b_down = b_down + b[5 + k]
            a_down = along_z(a_down, -1)
            b_up = along_z(b_up, 1)
            if k < 2:
                a_down = a_down + a[6 + k]
                b_up = b_up + b[2 - k]

    def joined(own, up, down):
        total = own.astype(jnp.float32) + up.astype(jnp.float32) + down.astype(jnp.float32)
        return total.astype(jnp.bfloat16)

    return jnp.concatenate([joined(a[0], a_up, a_down), joined(b[0], b_up, b_down)], axis=1)


def shift_sections(value, core_flip):
    sections, count = lax.axis_size("section"), lax.axis_size("tensor")
    pairs = [(s * count + t, (s - 1) * count + (t ^ core_flip)) for s in range(1, sections) for t in range(count)]
    return lax.ppermute(value, ("section", "tensor"), pairs)


def local(queries, key_rows, value_rows, out_grad, layer_input, query_weight, dion_basis, lengths):
    tokens, width = queries.shape[1:]
    tensor_index = lax.axis_index("tensor")
    z, core = tensor_index // 2, tensor_index % 2
    group_head = tensor_index * (width // HD) // GROUP
    info = jnp.stack([z, core, group_head]).astype(jnp.int32)
    half = D // 2

    own_columns = exchange_z(layer_input[0].reshape(CHUNK, ZN, D // ZN).transpose(1, 0, 2))
    w_other = swap_cores(lax.dynamic_slice_in_dim(query_weight[0], (1 - core) * half, half, 0))
    basis_other = swap_cores(dion_basis[0])
    other_columns = swap_cores(own_columns)
    by_core = jnp.stack([own_columns, other_columns], axis=1)
    by_core = jnp.where(core == 0, by_core, by_core[:, ::-1])
    columns = by_core.reshape(tokens, D // ZN)
    gram_part = dot_f32(own_columns.reshape(tokens // 2, D // ZN), columns, ((1,), (1,)))
    token_gram = jnp.sum(exchange_z(gram_part.reshape(ZN, CHUNK, tokens)), axis=0)

    token_ids = jnp.arange(tokens, dtype=jnp.int32)
    bound_two = lengths[0, 0] + lengths[0, 1]
    positions = jnp.where(token_ids < bound_two, token_ids, token_ids - lengths[0, 1]).astype(jnp.float32)
    freq_ids = jnp.arange(HD // 2, dtype=jnp.float32)
    angles = positions[:, None] * jnp.exp(-math.log(rope_base) * 2.0 * freq_ids / HD)[None, :]
    cosine, sine = jnp.cos(angles), jnp.sin(angles)
    cosine = jnp.concatenate([cosine, cosine], axis=1)
    sine = jnp.concatenate([sine, -sine], axis=1)
    query_grad = attention(info, lengths, cosine, sine, queries, out_grad, key_rows, value_rows)
    grad_other = swap_cores(query_grad)

    def own_rows(value):
        return lax.dynamic_index_in_dim(value.reshape(ZN, 2, CHUNK, width), core, 1, False).reshape(tokens // 2, width)

    part = dot_f32(own_rows(query_grad).astype(jnp.float32), dion_basis[0], ((1,), (0,)), highest)
    part += dot_f32(own_rows(grad_other).astype(jnp.float32), basis_other, ((1,), (0,)), highest)
    own_projected = jnp.sum(exchange_z(part.reshape(ZN, CHUNK, part.shape[1])), axis=0)
    projected = lax.all_gather(own_projected, "tensor", axis=0, tiled=True)
    mixed = lax.all_gather(dot_f32(token_gram, projected, ((1,), (0,)), highest), "tensor", axis=0, tiled=True)
    left_factor, right_factor = dion_factors(info, projected, mixed, columns, query_grad)

    partial = layer_partial(info, query_grad, grad_other, query_weight, w_other)
    parts = [partial[2 * CHUNK * r : 2 * CHUNK * (r + 1)] for r in range(ZN)]
    summed = tree_reduce_scatter(parts)
    from_own = shift_sections(summed[:CHUNK], 0)
    from_other = shift_sections(summed[CHUNK:], 1)
    upstream = jnp.where(
        core == 0,
        jnp.concatenate([from_own, from_other], axis=1),
        jnp.concatenate([from_other, from_own], axis=1),
    )
    return (upstream[None], left_factor, right_factor)


def solution(mesh):
    placed = (
        P("section", None, "tensor"),
        P("section", None, None),
        P("section", None, None),
        P("section", None, "tensor"),
        P("section", "tensor", None),
        P("section", None, "tensor"),
        P("section", "tensor", None),
        P("section", None),
    )
    return jax.shard_map(
        local,
        mesh=mesh,
        in_specs=placed,
        out_specs=(
            P("section", "tensor", None),
            P("section", "tensor", None),
            P("section", "tensor", None),
        ),
        check_vma=False,
    )
```

```python
import functools
import math

import jax
import jax.numpy as jnp
from jax import lax
from jax.experimental import pallas as pl
from jax.experimental.pallas import tpu as pltpu
from jax.sharding import PartitionSpec as P

D = 8192
HD = 128
GROUP = 8
ZN = 8
CHUNK = 32

rope_base = 500000.0
highest = lax.Precision.HIGHEST
z_groups = [[2 * z + core for z in range(ZN)] for core in range(2)]


def dot_f32(a, b, dims, precision=None):
    return lax.dot_general(a, b, (dims, ((), ())), precision=precision, preferred_element_type=jnp.float32)


def attention_kernel(info, lens, q_ref, g_ref, k_ref, v_ref, out_ref, bias, cos_ref, sin_ref):
    block = 256
    tokens, width = q_ref.shape[1:]
    core = info[1]
    scale = 1.0 / math.sqrt(HD)

    @pl.when(pl.program_id(0) == 0)
    def _():
        bound_one = lens[0, 0]
        bound_two = lens[0, 0] + lens[0, 1]
        i = lax.broadcasted_iota(jnp.int32, bias.shape, 0)
        j = lax.broadcasted_iota(jnp.int32, bias.shape, 1)
        crossed = (i >= bound_two) & (j >= bound_one) & (j < bound_two)
        visible = (j <= i) & jnp.logical_not(crossed)
        bias[...] = jnp.where(visible, 0.0, -jnp.inf)
        token = lax.broadcasted_iota(jnp.int32, cos_ref.shape, 0)
        position = jnp.where(token < bound_two, token, token - lens[0, 1]).astype(jnp.float32)
        lane = lax.broadcasted_iota(jnp.int32, cos_ref.shape, 1)
        freq_ids = jnp.where(lane < HD // 2, lane, lane - HD // 2).astype(jnp.float32)
        angle = position * jnp.exp(-math.log(rope_base) * 2.0 * freq_ids / HD)
        cos_ref[...] = jnp.cos(angle)
        sin_ref[...] = jnp.where(lane < HD // 2, 1.0, -1.0) * jnp.sin(angle)

    for row in range(0, tokens, block):
        keys = row + block
        here = slice(row, row + block)
        k = k_ref[0, :keys, :]
        v = v_ref[0, :keys, :]
        for head in range(0, width, HD):
            lanes = slice(head, head + HD)
            s = dot_f32(q_ref[0, here, lanes], k, ((1,), (1,))) + bias[here, :keys]
            dp = dot_f32(g_ref[0, here, lanes], v, ((1,), (1,)))
            e = jnp.exp2((s - jnp.max(s, axis=-1, keepdims=True)) * (scale * math.log2(math.e)))
            w = e * (1.0 / jnp.sum(e, axis=-1, keepdims=True))
            low = w.astype(jnp.bfloat16).astype(jnp.float32)
            out_dot = jnp.sum(low * dp, axis=-1, keepdims=True)
            ds = (w * (dp - out_dot)).astype(jnp.bfloat16)
            r = dot_f32(ds, k, ((1,), (0,))) * scale
            turned = jnp.concatenate([r[:, HD // 2 :], r[:, : HD // 2]], axis=1)
            r = (r * cos_ref[here, :] + turned * sin_ref[here, :]).astype(jnp.bfloat16)
            for n in range(block // CHUNK):
                chip, side = divmod(row // CHUNK + n, 2)
                target = pl.multiple_of((core ^ side) * (tokens // 2) + chip * CHUNK, CHUNK)
                out_ref[pl.ds(target, CHUNK), lanes] = r[n * CHUNK : (n + 1) * CHUNK, :]


def attention(info, lengths, queries, out_grad, key_rows, value_rows):
    tokens, width = queries.shape[1:]
    heads = width // HD
    pair = 2 * HD
    head_block = pl.BlockSpec((1, tokens, pair), lambda h, info, lens: (0, 0, h))
    kv_block = pl.BlockSpec((1, tokens, HD), lambda h, info, lens: (0, 0, info[2]))
    return pl.pallas_call(
        attention_kernel,
        out_shape=jax.ShapeDtypeStruct((tokens, width), jnp.bfloat16),
        grid_spec=pltpu.PrefetchScalarGridSpec(
            num_scalar_prefetch=2,
            grid=(width // pair,),
            in_specs=[head_block, head_block, kv_block, kv_block],
            out_specs=pl.BlockSpec((tokens, pair), lambda h, info, lens: (0, h)),
            scratch_shapes=[pltpu.VMEM((tokens, tokens), jnp.float32)] + [pltpu.VMEM((tokens, HD), jnp.float32)] * 2,
        ),
        compiler_params=pltpu.CompilerParams(vmem_limit_bytes=58 << 20),
        cost_estimate=pl.CostEstimate(
            flops=heads * 4 * 2 * tokens * tokens * HD, bytes_accessed=4 << 20, transcendentals=heads * tokens * tokens
        ),
        name="attention_backward",
    )(info, lengths, queries, out_grad, key_rows, value_rows)


up_cars = ((4, 3, 2, 1), (3, 2, 1, 0))
down_cars = ((5, 6, 7, 0), (4, 5, 6, 7))


def layer_kernel(info, mine_ref, other_ref, w_mine_ref, w_other_ref, up_ref, down_ref, rest_ref, rows_a, rows_b):
    z = info[0]
    step, steps = pl.program_id(0), pl.num_programs(0)
    cars = up_ref.shape[0]

    @pl.when(step == 0)
    def _():
        for half in range(2):
            for place, chip in enumerate((up_cars[half][0], down_cars[half][0]) + up_cars[half][1:] + down_cars[half][1:]):
                start = lax.rem(z + chip, ZN) * CHUNK
                for side in range(2):
                    target = slice((2 * place + side) * CHUNK, (2 * place + side + 1) * CHUNK)
                    rows_a[half, target, :] = mine_ref[pl.ds(pl.multiple_of(start + side * ZN * CHUNK, CHUNK), CHUNK), :]
                    start_b = pl.multiple_of(start + (1 - side) * ZN * CHUNK, CHUNK)
                    rows_b[half, target, :] = other_ref[pl.ds(start_b, CHUNK), :]

    half = lax.div(2 * step, steps)
    total = dot_f32(rows_a[half], w_mine_ref[0], ((1,), (1,)))
    total += dot_f32(rows_b[half], w_other_ref[0], ((1,), (1,)))
    total = total.astype(jnp.bfloat16)
    up_ref[...] = total[:cars]
    down_ref[...] = total[cars : 2 * cars]
    rest_ref[...] = total[2 * cars :]


def layer_partial(info, mine, other, w_mine, w_other):
    tokens, width = mine.shape
    columns = w_other.shape[1] // 2
    tile = 1024
    steps = columns // tile
    rows = [2 * CHUNK, 2 * CHUNK, tokens - 4 * CHUNK]
    whole = pl.BlockSpec((tokens, width), lambda i, info: (0, 0))
    weight = pl.BlockSpec((1, tile, width), lambda i, info: (0, info[1] * steps + i, 0))
    return pl.pallas_call(
        layer_kernel,
        out_shape=[jax.ShapeDtypeStruct((count, columns), jnp.bfloat16) for count in rows],
        grid_spec=pltpu.PrefetchScalarGridSpec(
            num_scalar_prefetch=1,
            grid=(steps,),
            in_specs=[whole, whole, weight, weight],
            out_specs=[pl.BlockSpec((count, tile), lambda i, info: (0, i)) for count in rows],
            scratch_shapes=[pltpu.VMEM((2, tokens, width), jnp.bfloat16)] * 2,
        ),
        compiler_params=pltpu.CompilerParams(vmem_limit_bytes=56 << 20),
        cost_estimate=pl.CostEstimate(
            flops=4 * tokens * width * columns, bytes_accessed=4 * width * columns + (2 << 20), transcendentals=0
        ),
        name="layer_partial",
    )(info, mine, other, w_mine, w_other)


def split_three(value):
    high = value.astype(jnp.bfloat16)
    rest = value - high.astype(jnp.float32)
    middle = rest.astype(jnp.bfloat16)
    low = (rest - middle.astype(jnp.float32)).astype(jnp.bfloat16)
    return high, middle, low


def times_exact(narrow, wide):
    parts = [dot_f32(narrow, part, ((0,), (0,))) for part in split_three(wide)]
    return parts[0] + (parts[1] + parts[2])


def parts_kernel(mine_ref, other_ref, basis_ref, basis_other_ref, x_ref, x_other_ref, out_ref):
    rows, rank = mine_ref.shape[0], basis_ref.shape[2]
    total = None
    for grad, basis in ((mine_ref, basis_ref), (other_ref, basis_other_ref)):
        for piece in split_three(basis[0]):
            term = dot_f32(grad[...], piece, ((1,), (0,)))
            total = term if total is None else total + term
    out_ref[:, :rank] = total
    out_ref[:, rank : rank + rows] = dot_f32(x_ref[...], x_ref[...], ((1,), (1,)))
    out_ref[:, rank + rows :] = dot_f32(x_ref[...], x_other_ref[...], ((1,), (1,)))


def chip_parts(mine, other, basis, basis_other, inputs, inputs_other):
    rows = inputs.shape[0]
    width, rank = basis.shape[1:]
    upper = pl.BlockSpec((rows, width), lambda i: (0, 0))
    lower = pl.BlockSpec((rows, width), lambda i: (1, 0))
    whole = [pl.BlockSpec(value.shape, lambda i, n=value.ndim: (0,) * n) for value in (basis, basis_other, inputs, inputs_other)]
    return pl.pallas_call(
        parts_kernel,
        out_shape=jax.ShapeDtypeStruct((rows, rank + 2 * rows), jnp.float32),
        grid=(1,),
        in_specs=[upper, lower] + whole,
        out_specs=pl.BlockSpec((rows, rank + 2 * rows), lambda i: (0, 0)),
        compiler_params=pltpu.CompilerParams(vmem_limit_bytes=40 << 20),
        cost_estimate=pl.CostEstimate(flops=1 << 30, bytes_accessed=4 << 20, transcendentals=0),
        name="chip_parts",
    )(mine, other, basis, basis_other, inputs, inputs_other)


def lower_inverse(block):
    size = block.shape[0]
    width = 2 * size
    rows = lax.broadcasted_iota(jnp.int32, (size, size), 0)
    cols = lax.broadcasted_iota(jnp.int32, (size, size), 1)
    sub = lax.broadcasted_iota(jnp.int32, (8, width), 0)
    both = jnp.concatenate([block, (rows == cols).astype(jnp.float32)], axis=1)
    groups = [both[8 * n : 8 * n + 8, :] for n in range(size // 8)]
    pivots = []
    for own in range(size // 8):
        live = range(own, size // 8)
        spread = [
            {n: jnp.broadcast_to(groups[n][:, 8 * own + i : 8 * own + i + 1], (8, width)) for n in live} for i in range(8)
        ]
        for i in range(8):
            column = spread[i]
            pivot = column[own][i : i + 1, :]
            pivots.append(pivot[:, :1])
            inverse = 1.0 / pivot
            below = dict(column)
            below[own] = jnp.where(sub > i, column[own], 0.0)
            for later in range(i + 1, 8):
                factor = column[own][later : later + 1, :] * inverse
                for n in live:
                    spread[later][n] = spread[later][n] - below[n] * factor
            scaled = groups[own][i : i + 1, :] * inverse
            for n in live:
                groups[n] = groups[n] - below[n] * scaled
    done = jnp.concatenate(groups, axis=0)
    return done[:, size:] * (1.0 / jnp.sqrt(jnp.concatenate(pivots, axis=0)))


def dion_kernel(info, own_ref, other_ref, x_ref, x_other_ref, g_ref, left_ref, right_ref, work):
    rows = own_ref.shape[0]
    rank = left_ref.shape[2]
    size = 64
    p = jnp.concatenate([own_ref[:, :rank], other_ref[:, :rank]], axis=0)
    m_own = dot_f32(own_ref[:, rank:], p, ((1,), (0,)), highest)
    m_other = dot_f32(other_ref[:, rank + rows :], p[:rows], ((1,), (0,)), highest)
    m_other += dot_f32(other_ref[:, rank : rank + rows], p[rows:], ((1,), (0,)), highest)
    m = jnp.concatenate([m_own, m_other], axis=0)
    work[:, :rank] = dot_f32(p, m, ((0,), (0,)), highest)
    row_ids = lax.broadcasted_iota(jnp.int32, (rank, rank), 0)
    col_ids = lax.broadcasted_iota(jnp.int32, (rank, rank), 1)
    work[:, rank:] = (row_ids == col_ids).astype(jnp.float32)
    for start in range(0, rank, size):
        here = slice(start, start + size)
        strip = dot_f32(lower_inverse(work[here, here]), work[here, :], ((1,), (0,)), highest)
        work[here, :] = strip
        if start + size < rank:
            work[start + size :, :] -= dot_f32(strip[:, start + size : rank], strip, ((0,), (0,)), highest)
    inverse = work[:, rank:]
    left_mix = dot_f32(p, inverse, ((1,), (1,)), highest) * math.sqrt(D)
    left_ref[0] = times_exact(x_ref[...], left_mix[:rows]) + times_exact(x_other_ref[...], left_mix[rows:])
    right_mix = dot_f32(m, inverse, ((1,), (1,)), highest)
    right_ref[0] = times_exact(g_ref[...], right_mix)


def dion_factors(info, own, other, inputs, inputs_other, query_grad, rank):
    tokens, width = query_grad.shape
    whole = pl.BlockSpec(own.shape, lambda i, info: (0, 0))
    columns = pl.BlockSpec((tokens // 2, width), lambda i, info: (0, info[1]))
    result = pl.BlockSpec((1, width, rank), lambda i, info: (0, 0, 0))
    return pl.pallas_call(
        dion_kernel,
        out_shape=[jax.ShapeDtypeStruct((1, width, rank), jnp.float32)] * 2,
        grid_spec=pltpu.PrefetchScalarGridSpec(
            num_scalar_prefetch=1,
            grid=(1,),
            in_specs=[whole, whole, columns, columns, pl.BlockSpec((tokens, width), lambda i, info: (0, 0))],
            out_specs=[result, result],
            scratch_shapes=[pltpu.VMEM((rank, 2 * rank), jnp.float32)],
        ),
        compiler_params=pltpu.CompilerParams(vmem_limit_bytes=40 << 20),
        cost_estimate=pl.CostEstimate(flops=12 << 30, bytes_accessed=4 << 20, transcendentals=0),
        name="dion_factors",
    )(info, own, other, inputs, inputs_other, query_grad)


def after(value, other):
    return lax.optimization_barrier((value, other))[0]


def swap_cores(value):
    return lax.ppermute(value, "tensor", [(i, i ^ 1) for i in range(2 * ZN)])


def along_z(value, steps):
    count = 2 * ZN
    return lax.ppermute(value, "tensor", [(i, (i + 2 * steps) % count) for i in range(count)])


def exchange_z(value):
    return lax.all_to_all(value, "tensor", 0, 0, tiled=True, axis_index_groups=z_groups)


def shift_sections(value, core_flip):
    sections, count = lax.axis_size("section"), lax.axis_size("tensor")
    pairs = [(s * count + t, (s - 1) * count + (t ^ core_flip)) for s in range(1, sections) for t in range(count)]
    return lax.ppermute(value, ("section", "tensor"), pairs)


def local(queries, key_rows, value_rows, out_grad, layer_input, query_weight, dion_basis, lengths):
    tokens, width = queries.shape[1:]
    tensor_index = lax.axis_index("tensor")
    z, core = tensor_index // 2, tensor_index % 2
    group_head = tensor_index * (width // HD) // GROUP
    info = jnp.stack([z, core, group_head]).astype(jnp.int32)
    half_tokens = tokens // 2

    w_other = swap_cores(query_weight)
    basis_other = swap_cores(dion_basis)

    by_column = layer_input[0].reshape(CHUNK, ZN, D // ZN).transpose(1, 0, 2)
    own_columns = exchange_z(by_column).reshape(half_tokens, D // ZN)

    query_grad = attention(info, lengths, queries, out_grad, key_rows, value_rows)
    grad_other = swap_cores(query_grad)

    up, down, rest = layer_partial(info, query_grad, grad_other, query_weight, w_other)

    own_columns = after(own_columns, up)
    other_columns = swap_cores(own_columns)
    chip_part = chip_parts(query_grad, grad_other, dion_basis, basis_other, own_columns, other_columns)
    summands = exchange_z(chip_part.reshape(ZN, CHUNK, chip_part.shape[1]))
    rows = 2 * CHUNK
    up_rest = [rest[rows * n : rows * (n + 1)] for n in range(3)]
    down_rest = [rest[rows * (3 + n) : rows * (4 + n)] for n in range(3)]

    own = jnp.sum(summands, axis=0)
    own = jnp.broadcast_to(own[None], (ZN,) + own.shape)
    gathered = exchange_z(own).reshape(half_tokens, own.shape[2])
    gathered_other = swap_cores(gathered)
    for n in range(3):
        up, down = along_z(up, 1), along_z(down, -1)
        if n == 1:
            up, down = after((up, down), own)
        if n == 2:
            up, down = after((up, down), gathered)
        up, down = up + up_rest[n], down + down_rest[n]
    half = up.shape[1] // 2
    last_up, last_down = along_z(up[:, :half], 1), along_z(down[:, half:], -1)

    def total(a, b):
        return (a.astype(jnp.float32) + b.astype(jnp.float32)).astype(jnp.bfloat16)

    summed = jnp.concatenate([total(last_up, down[:, :half]), total(last_down, up[:, half:])], axis=1)
    left_factor, right_factor = dion_factors(
        info, gathered, after(gathered_other, summed), own_columns, other_columns, query_grad, dion_basis.shape[2]
    )

    from_own = shift_sections(summed[:CHUNK], 0)
    from_other = shift_sections(summed[CHUNK:], 1)
    from_own, from_other = after((from_own, from_other), left_factor)
    upstream = jnp.where(
        core == 0,
        jnp.concatenate([from_own, from_other], axis=1),
        jnp.concatenate([from_other, from_own], axis=1),
    )
    return (upstream[None], left_factor, right_factor)


def solution(mesh):
    placed = (
        P("section", None, "tensor"),
        P("section", None, None),
        P("section", None, None),
        P("section", None, "tensor"),
        P("section", "tensor", None),
        P("section", None, "tensor"),
        P("section", "tensor", None),
        P("section", None),
    )
    return jax.shard_map(
        local,
        mesh=mesh,
        in_specs=placed,
        out_specs=(
            P("section", "tensor", None),
            P("section", "tensor", None),
            P("section", "tensor", None),
        ),
        check_vma=False,
    )
```

```python
import functools
import math

import jax
import jax.numpy as jnp
from jax import lax
from jax.experimental import pallas as pl
from jax.experimental.pallas import tpu as pltpu
from jax.sharding import PartitionSpec as P

D = 8192
HD = 128
GROUP = 8
ZN = 8
CHUNK = 32

rope_base = 500000.0
highest = lax.Precision.HIGHEST
z_groups = [[2 * z + core for z in range(ZN)] for core in range(2)]


def dot_f32(a, b, dims, precision=None):
    return lax.dot_general(a, b, (dims, ((), ())), precision=precision, preferred_element_type=jnp.float32)


def attention_kernel(info, lens, q_ref, g_ref, k_ref, v_ref, out_ref, bias, cos_ref, sin_ref):
    block = 256
    tokens, width = q_ref.shape[1:]
    core = info[1]
    scale = 1.0 / math.sqrt(HD)

    @pl.when(pl.program_id(0) == 0)
    def _():
        bound_one = lens[0, 0]
        bound_two = lens[0, 0] + lens[0, 1]
        i = lax.broadcasted_iota(jnp.int32, bias.shape, 0)
        j = lax.broadcasted_iota(jnp.int32, bias.shape, 1)
        crossed = (i >= bound_two) & (j >= bound_one) & (j < bound_two)
        visible = (j <= i) & jnp.logical_not(crossed)
        bias[...] = jnp.where(visible, 0.0, -jnp.inf)
        token = lax.broadcasted_iota(jnp.int32, cos_ref.shape, 0)
        position = jnp.where(token < bound_two, token, token - lens[0, 1]).astype(jnp.float32)
        lane = lax.broadcasted_iota(jnp.int32, cos_ref.shape, 1)
        freq_ids = jnp.where(lane < HD // 2, lane, lane - HD // 2).astype(jnp.float32)
        angle = position * jnp.exp(-math.log(rope_base) * 2.0 * freq_ids / HD)
        cos_ref[...] = jnp.cos(angle)
        sin_ref[...] = jnp.where(lane < HD // 2, 1.0, -1.0) * jnp.sin(angle)

    for row in range(0, tokens, block):
        keys = row + block
        here = slice(row, row + block)
        k = k_ref[0, :keys, :]
        v = v_ref[0, :keys, :]
        for head in range(0, width, HD):
            lanes = slice(head, head + HD)
            s = dot_f32(q_ref[0, here, lanes], k, ((1,), (1,))) + bias[here, :keys]
            dp = dot_f32(g_ref[0, here, lanes], v, ((1,), (1,)))
            e = jnp.exp2((s - jnp.max(s, axis=-1, keepdims=True)) * (scale * math.log2(math.e)))
            w = e * (1.0 / jnp.sum(e, axis=-1, keepdims=True))
            low = w.astype(jnp.bfloat16).astype(jnp.float32)
            out_dot = jnp.sum(low * dp, axis=-1, keepdims=True)
            ds = (w * (dp - out_dot)).astype(jnp.bfloat16)
            r = dot_f32(ds, k, ((1,), (0,))) * scale
            turned = jnp.concatenate([r[:, HD // 2 :], r[:, : HD // 2]], axis=1)
            r = (r * cos_ref[here, :] + turned * sin_ref[here, :]).astype(jnp.bfloat16)
            for n in range(block // CHUNK):
                chip, side = divmod(row // CHUNK + n, 2)
                target = pl.multiple_of((core ^ side) * (tokens // 2) + chip * CHUNK, CHUNK)
                out_ref[pl.ds(target, CHUNK), lanes] = r[n * CHUNK : (n + 1) * CHUNK, :]


def attention(info, lengths, queries, out_grad, key_rows, value_rows):
    tokens, width = queries.shape[1:]
    heads = width // HD
    pair = 2 * HD
    head_block = pl.BlockSpec((1, tokens, pair), lambda h, info, lens: (0, 0, h))
    kv_block = pl.BlockSpec((1, tokens, HD), lambda h, info, lens: (0, 0, info[2]))
    return pl.pallas_call(
        attention_kernel,
        out_shape=jax.ShapeDtypeStruct((tokens, width), jnp.bfloat16),
        grid_spec=pltpu.PrefetchScalarGridSpec(
            num_scalar_prefetch=2,
            grid=(width // pair,),
            in_specs=[head_block, head_block, kv_block, kv_block],
            out_specs=pl.BlockSpec((tokens, pair), lambda h, info, lens: (0, h)),
            scratch_shapes=[pltpu.VMEM((tokens, tokens), jnp.float32)] + [pltpu.VMEM((tokens, HD), jnp.float32)] * 2,
        ),
        compiler_params=pltpu.CompilerParams(vmem_limit_bytes=58 << 20),
        cost_estimate=pl.CostEstimate(flops=1 << 20, bytes_accessed=1 << 20, transcendentals=0),
        name="attention_backward",
    )(info, lengths, queries, out_grad, key_rows, value_rows)


up_cars = ((4, 3, 2, 1), (3, 2, 1, 0))
down_cars = ((5, 6, 7, 0), (4, 5, 6, 7))


def layer_kernel(info, mine_ref, other_ref, w_mine_ref, w_other_ref, up_ref, down_ref, rest_ref, rows_a, rows_b):
    z = info[0]
    step, steps = pl.program_id(0), pl.num_programs(0)
    cars = up_ref.shape[0]

    @pl.when(step == 0)
    def _():
        for half in range(2):
            for place, chip in enumerate((up_cars[half][0], down_cars[half][0]) + up_cars[half][1:] + down_cars[half][1:]):
                start = lax.rem(z + chip, ZN) * CHUNK
                for side in range(2):
                    target = slice((2 * place + side) * CHUNK, (2 * place + side + 1) * CHUNK)
                    rows_a[half, target, :] = mine_ref[pl.ds(pl.multiple_of(start + side * ZN * CHUNK, CHUNK), CHUNK), :]
                    start_b = pl.multiple_of(start + (1 - side) * ZN * CHUNK, CHUNK)
                    rows_b[half, target, :] = other_ref[pl.ds(start_b, CHUNK), :]

    half = lax.div(2 * step, steps)
    total = dot_f32(rows_a[half], w_mine_ref[0], ((1,), (1,)))
    total += dot_f32(rows_b[half], w_other_ref[0], ((1,), (1,)))
    total = total.astype(jnp.bfloat16)
    up_ref[...] = total[:cars]
    down_ref[...] = total[cars : 2 * cars]
    rest_ref[...] = total[2 * cars :]


def layer_partial(info, mine, other, w_mine, w_other):
    tokens, width = mine.shape
    columns = w_other.shape[1] // 2
    tile = 1024
    steps = columns // tile
    rows = [2 * CHUNK, 2 * CHUNK, tokens - 4 * CHUNK]
    whole = pl.BlockSpec((tokens, width), lambda i, info: (0, 0))
    weight = pl.BlockSpec((1, tile, width), lambda i, info: (0, info[1] * steps + i, 0))
    return pl.pallas_call(
        layer_kernel,
        out_shape=[jax.ShapeDtypeStruct((count, columns), jnp.bfloat16) for count in rows],
        grid_spec=pltpu.PrefetchScalarGridSpec(
            num_scalar_prefetch=1,
            grid=(steps,),
            in_specs=[whole, whole, weight, weight],
            out_specs=[pl.BlockSpec((count, tile), lambda i, info: (0, i)) for count in rows],
            scratch_shapes=[pltpu.VMEM((2, tokens, width), jnp.bfloat16)] * 2,
        ),
        compiler_params=pltpu.CompilerParams(vmem_limit_bytes=56 << 20),
        cost_estimate=pl.CostEstimate(flops=1 << 20, bytes_accessed=1 << 20, transcendentals=0),
        name="layer_partial",
    )(info, mine, other, w_mine, w_other)


def split_three(value):
    high = value.astype(jnp.bfloat16)
    rest = value - high.astype(jnp.float32)
    middle = rest.astype(jnp.bfloat16)
    low = (rest - middle.astype(jnp.float32)).astype(jnp.bfloat16)
    return high, middle, low


def times_exact(narrow, wide):
    parts = [dot_f32(narrow, part, ((0,), (0,))) for part in split_three(wide)]
    return parts[0] + (parts[1] + parts[2])


def parts_kernel(mine_ref, other_ref, basis_ref, basis_other_ref, x_ref, x_other_ref, out_ref):
    rows, rank = mine_ref.shape[0], basis_ref.shape[2]
    total = None
    for grad, basis in ((mine_ref, basis_ref), (other_ref, basis_other_ref)):
        for piece in split_three(basis[0]):
            term = dot_f32(grad[...], piece, ((1,), (0,)))
            total = term if total is None else total + term
    out_ref[:, :rank] = total
    out_ref[:, rank : rank + rows] = dot_f32(x_ref[...], x_ref[...], ((1,), (1,)))
    out_ref[:, rank + rows :] = dot_f32(x_ref[...], x_other_ref[...], ((1,), (1,)))


def chip_parts(mine, other, basis, basis_other, inputs, inputs_other):
    rows = inputs.shape[0]
    width, rank = basis.shape[1:]
    upper = pl.BlockSpec((rows, width), lambda i: (0, 0))
    lower = pl.BlockSpec((rows, width), lambda i: (1, 0))
    whole = [pl.BlockSpec(value.shape, lambda i, n=value.ndim: (0,) * n) for value in (basis, basis_other, inputs, inputs_other)]
    return pl.pallas_call(
        parts_kernel,
        out_shape=jax.ShapeDtypeStruct((rows, rank + 2 * rows), jnp.float32),
        grid=(1,),
        in_specs=[upper, lower] + whole,
        out_specs=pl.BlockSpec((rows, rank + 2 * rows), lambda i: (0, 0)),
        compiler_params=pltpu.CompilerParams(vmem_limit_bytes=40 << 20),
        cost_estimate=pl.CostEstimate(flops=1 << 30, bytes_accessed=4 << 20, transcendentals=0),
        name="chip_parts",
    )(mine, other, basis, basis_other, inputs, inputs_other)


def lower_inverse(block):
    size = block.shape[0]
    width = 2 * size
    rows = lax.broadcasted_iota(jnp.int32, (size, size), 0)
    cols = lax.broadcasted_iota(jnp.int32, (size, size), 1)
    sub = lax.broadcasted_iota(jnp.int32, (8, width), 0)
    both = jnp.concatenate([block, (rows == cols).astype(jnp.float32)], axis=1)
    groups = [both[8 * n : 8 * n + 8, :] for n in range(size // 8)]
    pivots = []
    for own in range(size // 8):
        live = range(own, size // 8)
        spread = [
            {n: jnp.broadcast_to(groups[n][:, 8 * own + i : 8 * own + i + 1], (8, width)) for n in live} for i in range(8)
        ]
        for i in range(8):
            column = spread[i]
            pivot = column[own][i : i + 1, :]
            pivots.append(pivot[:, :1])
            inverse = 1.0 / pivot
            below = dict(column)
            below[own] = jnp.where(sub > i, column[own], 0.0)
            for later in range(i + 1, 8):
                factor = column[own][later : later + 1, :] * inverse
                for n in live:
                    spread[later][n] = spread[later][n] - below[n] * factor
            scaled = groups[own][i : i + 1, :] * inverse
            for n in live:
                groups[n] = groups[n] - below[n] * scaled
    done = jnp.concatenate(groups, axis=0)
    return done[:, size:] * (1.0 / jnp.sqrt(jnp.concatenate(pivots, axis=0)))


def dion_kernel(own_ref, other_ref, left_ref, right_ref, work):
    rows = own_ref.shape[0]
    rank = left_ref.shape[1]
    size = 64
    p = jnp.concatenate([own_ref[:, :rank], other_ref[:, :rank]], axis=0)
    m_own = dot_f32(own_ref[:, rank:], p, ((1,), (0,)), highest)
    m_other = dot_f32(other_ref[:, rank + rows :], p[:rows], ((1,), (0,)), highest)
    m_other += dot_f32(other_ref[:, rank : rank + rows], p[rows:], ((1,), (0,)), highest)
    m = jnp.concatenate([m_own, m_other], axis=0)
    work[:, :rank] = dot_f32(p, m, ((0,), (0,)), highest)
    row_ids = lax.broadcasted_iota(jnp.int32, (rank, rank), 0)
    col_ids = lax.broadcasted_iota(jnp.int32, (rank, rank), 1)
    work[:, rank:] = (row_ids == col_ids).astype(jnp.float32)
    for start in range(0, rank, size):
        here = slice(start, start + size)
        strip = dot_f32(lower_inverse(work[here, here]), work[here, :], ((1,), (0,)), highest)
        work[here, :] = strip
        if start + size < rank:
            work[start + size :, :] -= dot_f32(strip[:, start + size : rank], strip, ((0,), (0,)), highest)
    inverse = work[:, rank:]
    left_ref[...] = dot_f32(p, inverse, ((1,), (1,)), highest) * math.sqrt(D)
    right_ref[...] = dot_f32(m, inverse, ((1,), (1,)), highest)


def dion_mixes(own, other, rank):
    tokens = 2 * own.shape[0]
    return pl.pallas_call(
        dion_kernel,
        out_shape=[jax.ShapeDtypeStruct((tokens, rank), jnp.float32)] * 2,
        scratch_shapes=[pltpu.VMEM((rank, 2 * rank), jnp.float32)],
        compiler_params=pltpu.CompilerParams(vmem_limit_bytes=40 << 20),
        cost_estimate=pl.CostEstimate(flops=10 << 30, bytes_accessed=4 << 20, transcendentals=0),
        name="dion_mixes",
    )(own, other)


def factors_kernel(info, left_mix, right_mix, x_ref, x_other_ref, g_ref, left_ref, right_ref):
    rows = x_ref.shape[0]
    left_ref[0] = times_exact(x_ref[...], left_mix[:rows, :]) + times_exact(x_other_ref[...], left_mix[rows:, :])
    right_ref[0] = times_exact(g_ref[...], right_mix[...])


def dion_factors(info, left_mix, right_mix, inputs, inputs_other, query_grad):
    tokens, width = query_grad.shape
    rank = left_mix.shape[1]
    mix = pl.BlockSpec((tokens, rank), lambda i, info: (0, 0))
    columns = pl.BlockSpec((tokens // 2, width), lambda i, info: (0, info[1]))
    result = pl.BlockSpec((1, width, rank), lambda i, info: (0, 0, 0))
    return pl.pallas_call(
        factors_kernel,
        out_shape=[jax.ShapeDtypeStruct((1, width, rank), jnp.float32)] * 2,
        grid_spec=pltpu.PrefetchScalarGridSpec(
            num_scalar_prefetch=1,
            grid=(1,),
            in_specs=[mix, mix, columns, columns, pl.BlockSpec((tokens, width), lambda i, info: (0, 0))],
            out_specs=[result, result],
        ),
        compiler_params=pltpu.CompilerParams(vmem_limit_bytes=40 << 20),
        cost_estimate=pl.CostEstimate(flops=2 << 30, bytes_accessed=4 << 20, transcendentals=0),
        name="dion_factors",
    )(info, left_mix, right_mix, inputs, inputs_other, query_grad)


def after(value, other):
    return lax.optimization_barrier((value, other))[0]


def swap_cores(value):
    return lax.ppermute(value, "tensor", [(i, i ^ 1) for i in range(2 * ZN)])


def along_z(value, steps):
    count = 2 * ZN
    return lax.ppermute(value, "tensor", [(i, (i + 2 * steps) % count) for i in range(count)])


def exchange_z(value):
    return lax.all_to_all(value, "tensor", 0, 0, tiled=True, axis_index_groups=z_groups)


def shift_sections(value, core_flip):
    sections, count = lax.axis_size("section"), lax.axis_size("tensor")
    pairs = [(s * count + t, (s - 1) * count + (t ^ core_flip)) for s in range(1, sections) for t in range(count)]
    return lax.ppermute(value, ("section", "tensor"), pairs)


def local(queries, key_rows, value_rows, out_grad, layer_input, query_weight, dion_basis, lengths):
    tokens, width = queries.shape[1:]
    tensor_index = lax.axis_index("tensor")
    z, core = tensor_index // 2, tensor_index % 2
    group_head = tensor_index * (width // HD) // GROUP
    info = jnp.stack([z, core, group_head]).astype(jnp.int32)
    half_tokens = tokens // 2

    w_other = swap_cores(query_weight)
    basis_other = swap_cores(dion_basis)

    by_column = layer_input[0].reshape(CHUNK, ZN, D // ZN).transpose(1, 0, 2)
    own_columns = exchange_z(by_column).reshape(half_tokens, D // ZN)

    query_grad = attention(info, lengths, queries, out_grad, key_rows, value_rows)
    grad_other = swap_cores(query_grad)

    up, down, rest = layer_partial(info, query_grad, grad_other, query_weight, w_other)

    own_columns = after(own_columns, up)
    other_columns = swap_cores(own_columns)
    chip_part = chip_parts(query_grad, grad_other, dion_basis, basis_other, own_columns, other_columns)
    summands = exchange_z(chip_part.reshape(ZN, CHUNK, chip_part.shape[1]))
    rows = 2 * CHUNK
    up_rest = [rest[rows * n : rows * (n + 1)] for n in range(3)]
    down_rest = [rest[rows * (3 + n) : rows * (4 + n)] for n in range(3)]

    own = jnp.sum(summands, axis=0)
    own = jnp.broadcast_to(own[None], (ZN,) + own.shape)
    gathered = exchange_z(own).reshape(half_tokens, own.shape[2])
    gathered_other = swap_cores(gathered)
    for n in range(3):
        up, down = along_z(up, 1), along_z(down, -1)
        if n == 1:
            up, down = after((up, down), own)
        if n == 2:
            up, down = after((up, down), gathered)
        up, down = up + up_rest[n], down + down_rest[n]
    half = up.shape[1] // 2
    last_up, last_down = along_z(up[:, :half], 1), along_z(down[:, half:], -1)

    left_mix, right_mix = dion_mixes(gathered, gathered_other, dion_basis.shape[2])

    def total(a, b):
        return (a.astype(jnp.float32) + b.astype(jnp.float32)).astype(jnp.bfloat16)

    last_up, last_down = after((last_up, last_down), left_mix)
    summed = jnp.concatenate([total(last_up, down[:, :half]), total(last_down, up[:, half:])], axis=1)

    from_own = shift_sections(summed[:CHUNK], 0)
    from_other = shift_sections(summed[CHUNK:], 1)
    left_factor, right_factor = dion_factors(
        info, after(left_mix, summed), right_mix, own_columns, other_columns, query_grad
    )
    from_own, from_other = after((from_own, from_other), left_factor)
    upstream = jnp.where(
        core == 0,
        jnp.concatenate([from_own, from_other], axis=1),
        jnp.concatenate([from_other, from_own], axis=1),
    )
    return (upstream[None], left_factor, right_factor)


def solution(mesh):
    placed = (
        P("section", None, "tensor"),
        P("section", None, None),
        P("section", None, None),
        P("section", None, "tensor"),
        P("section", "tensor", None),
        P("section", None, "tensor"),
        P("section", "tensor", None),
        P("section", None),
    )
    return jax.shard_map(
        local,
        mesh=mesh,
        in_specs=placed,
        out_specs=(
            P("section", "tensor", None),
            P("section", "tensor", None),
            P("section", "tensor", None),
        ),
        check_vma=False,
    )
```

```python
import functools
import math

import jax
import jax.numpy as jnp
from jax import lax
from jax.experimental import pallas as pl
from jax.experimental.pallas import tpu as pltpu
from jax.sharding import PartitionSpec as P

D = 8192
HD = 128
GROUP = 8
ZN = 8
CHUNK = 32

rope_base = 500000.0
highest = lax.Precision.HIGHEST
z_groups = [[2 * z + core for z in range(ZN)] for core in range(2)]


def dot_f32(a, b, dims, precision=None):
    return lax.dot_general(a, b, (dims, ((), ())), precision=precision, preferred_element_type=jnp.float32)


def attention_kernel(info, lens, q_ref, g_ref, k_ref, v_ref, out_ref, bias, cos_ref, sin_ref):
    block = 256
    tokens, width = q_ref.shape[1:]
    core = info[1]
    scale = 1.0 / math.sqrt(HD)

    @pl.when(pl.program_id(0) == 0)
    def _():
        bound_one = lens[0, 0]
        bound_two = lens[0, 0] + lens[0, 1]
        i = lax.broadcasted_iota(jnp.int32, bias.shape, 0)
        j = lax.broadcasted_iota(jnp.int32, bias.shape, 1)
        crossed = (i >= bound_two) & (j >= bound_one) & (j < bound_two)
        visible = (j <= i) & jnp.logical_not(crossed)
        bias[...] = jnp.where(visible, 0.0, -jnp.inf)
        token = lax.broadcasted_iota(jnp.int32, cos_ref.shape, 0)
        position = jnp.where(token < bound_two, token, token - lens[0, 1]).astype(jnp.float32)
        lane = lax.broadcasted_iota(jnp.int32, cos_ref.shape, 1)
        freq_ids = jnp.where(lane < HD // 2, lane, lane - HD // 2).astype(jnp.float32)
        angle = position * jnp.exp(-math.log(rope_base) * 2.0 * freq_ids / HD)
        cos_ref[...] = jnp.cos(angle)
        sin_ref[...] = jnp.where(lane < HD // 2, 1.0, -1.0) * jnp.sin(angle)

    for row in range(0, tokens, block):
        keys = row + block
        here = slice(row, row + block)
        k = k_ref[0, :keys, :]
        v = v_ref[0, :keys, :]
        for head in range(0, width, HD):
            lanes = slice(head, head + HD)
            s = dot_f32(q_ref[0, here, lanes], k, ((1,), (1,))) + bias[here, :keys]
            dp = dot_f32(g_ref[0, here, lanes], v, ((1,), (1,)))
            e = jnp.exp2((s - jnp.max(s, axis=-1, keepdims=True)) * (scale * math.log2(math.e)))
            w = e * (1.0 / jnp.sum(e, axis=-1, keepdims=True))
            low = w.astype(jnp.bfloat16).astype(jnp.float32)
            out_dot = jnp.sum(low * dp, axis=-1, keepdims=True)
            ds = (w * (dp - out_dot)).astype(jnp.bfloat16)
            r = dot_f32(ds, k, ((1,), (0,))) * scale
            turned = jnp.concatenate([r[:, HD // 2 :], r[:, : HD // 2]], axis=1)
            r = (r * cos_ref[here, :] + turned * sin_ref[here, :]).astype(jnp.bfloat16)
            for n in range(block // CHUNK):
                chip, side = divmod(row // CHUNK + n, 2)
                target = pl.multiple_of((core ^ side) * (tokens // 2) + chip * CHUNK, CHUNK)
                out_ref[pl.ds(target, CHUNK), lanes] = r[n * CHUNK : (n + 1) * CHUNK, :]


def attention(info, lengths, queries, out_grad, key_rows, value_rows):
    tokens, width = queries.shape[1:]
    heads = width // HD
    pair = 2 * HD
    head_block = pl.BlockSpec((1, tokens, pair), lambda h, info, lens: (0, 0, h))
    kv_block = pl.BlockSpec((1, tokens, HD), lambda h, info, lens: (0, 0, info[2]))
    return pl.pallas_call(
        attention_kernel,
        out_shape=jax.ShapeDtypeStruct((tokens, width), jnp.bfloat16),
        grid_spec=pltpu.PrefetchScalarGridSpec(
            num_scalar_prefetch=2,
            grid=(width // pair,),
            in_specs=[head_block, head_block, kv_block, kv_block],
            out_specs=pl.BlockSpec((tokens, pair), lambda h, info, lens: (0, h)),
            scratch_shapes=[pltpu.VMEM((tokens, tokens), jnp.float32)] + [pltpu.VMEM((tokens, HD), jnp.float32)] * 2,
        ),
        compiler_params=pltpu.CompilerParams(vmem_limit_bytes=58 << 20),
        cost_estimate=pl.CostEstimate(flops=1 << 20, bytes_accessed=1 << 20, transcendentals=0),
        name="attention_backward",
    )(info, lengths, queries, out_grad, key_rows, value_rows)


up_cars = ((4, 3, 2, 1), (3, 2, 1, 0))
down_cars = ((5, 6, 7, 0), (4, 5, 6, 7))


def layer_kernel(info, mine_ref, other_ref, w_mine_ref, w_other_ref, up_ref, down_ref, rest_ref, rows_a, rows_b):
    z = info[0]
    step, steps = pl.program_id(0), pl.num_programs(0)
    cars = up_ref.shape[0]

    @pl.when(step == 0)
    def _():
        for half in range(2):
            for place, chip in enumerate((up_cars[half][0], down_cars[half][0]) + up_cars[half][1:] + down_cars[half][1:]):
                start = lax.rem(z + chip, ZN) * CHUNK
                for side in range(2):
                    target = slice((2 * place + side) * CHUNK, (2 * place + side + 1) * CHUNK)
                    rows_a[half, target, :] = mine_ref[pl.ds(pl.multiple_of(start + side * ZN * CHUNK, CHUNK), CHUNK), :]
                    start_b = pl.multiple_of(start + (1 - side) * ZN * CHUNK, CHUNK)
                    rows_b[half, target, :] = other_ref[pl.ds(start_b, CHUNK), :]

    half = lax.div(2 * step, steps)
    total = dot_f32(rows_a[half], w_mine_ref[0], ((1,), (1,)))
    total += dot_f32(rows_b[half], w_other_ref[0], ((1,), (1,)))
    total = total.astype(jnp.bfloat16)
    up_ref[...] = total[:cars]
    down_ref[...] = total[cars : 2 * cars]
    rest_ref[...] = total[2 * cars :]


def layer_partial(info, mine, other, w_mine, w_other):
    tokens, width = mine.shape
    columns = w_other.shape[1] // 2
    tile = 1024
    steps = columns // tile
    rows = [2 * CHUNK, 2 * CHUNK, tokens - 4 * CHUNK]
    whole = pl.BlockSpec((tokens, width), lambda i, info: (0, 0))
    weight = pl.BlockSpec((1, tile, width), lambda i, info: (0, info[1] * steps + i, 0))
    return pl.pallas_call(
        layer_kernel,
        out_shape=[jax.ShapeDtypeStruct((count, columns), jnp.bfloat16) for count in rows],
        grid_spec=pltpu.PrefetchScalarGridSpec(
            num_scalar_prefetch=1,
            grid=(steps,),
            in_specs=[whole, whole, weight, weight],
            out_specs=[pl.BlockSpec((count, tile), lambda i, info: (0, i)) for count in rows],
            scratch_shapes=[pltpu.VMEM((2, tokens, width), jnp.bfloat16)] * 2,
        ),
        compiler_params=pltpu.CompilerParams(vmem_limit_bytes=56 << 20),
        cost_estimate=pl.CostEstimate(flops=1 << 20, bytes_accessed=1 << 20, transcendentals=0),
        name="layer_partial",
    )(info, mine, other, w_mine, w_other)


def split_three(value):
    high = value.astype(jnp.bfloat16)
    rest = value - high.astype(jnp.float32)
    middle = rest.astype(jnp.bfloat16)
    low = (rest - middle.astype(jnp.float32)).astype(jnp.bfloat16)
    return high, middle, low


def times_exact(narrow, wide):
    parts = [dot_f32(narrow, part, ((0,), (0,))) for part in split_three(wide)]
    return parts[0] + (parts[1] + parts[2])


def parts_kernel(mine_ref, other_ref, basis_ref, basis_other_ref, x_ref, x_other_ref, out_ref):
    rows, rank = mine_ref.shape[0], basis_ref.shape[2]
    total = None
    for grad, basis in ((mine_ref, basis_ref), (other_ref, basis_other_ref)):
        for piece in split_three(basis[0]):
            term = dot_f32(grad[...], piece, ((1,), (0,)))
            total = term if total is None else total + term
    out_ref[:, :rank] = total
    out_ref[:, rank : rank + rows] = dot_f32(x_ref[...], x_ref[...], ((1,), (1,)))
    out_ref[:, rank + rows :] = dot_f32(x_ref[...], x_other_ref[...], ((1,), (1,)))


def chip_parts(mine, other, basis, basis_other, inputs, inputs_other):
    rows = inputs.shape[0]
    width, rank = basis.shape[1:]
    upper = pl.BlockSpec((rows, width), lambda i: (0, 0))
    lower = pl.BlockSpec((rows, width), lambda i: (1, 0))
    whole = [pl.BlockSpec(value.shape, lambda i, n=value.ndim: (0,) * n) for value in (basis, basis_other, inputs, inputs_other)]
    return pl.pallas_call(
        parts_kernel,
        out_shape=jax.ShapeDtypeStruct((rows, rank + 2 * rows), jnp.float32),
        grid=(1,),
        in_specs=[upper, lower] + whole,
        out_specs=pl.BlockSpec((rows, rank + 2 * rows), lambda i: (0, 0)),
        compiler_params=pltpu.CompilerParams(vmem_limit_bytes=40 << 20),
        cost_estimate=pl.CostEstimate(flops=1 << 30, bytes_accessed=4 << 20, transcendentals=0),
        name="chip_parts",
    )(mine, other, basis, basis_other, inputs, inputs_other)


def lower_inverse(block):
    size = block.shape[0]
    width = 2 * size
    rows = lax.broadcasted_iota(jnp.int32, (size, size), 0)
    cols = lax.broadcasted_iota(jnp.int32, (size, size), 1)
    sub = lax.broadcasted_iota(jnp.int32, (8, width), 0)
    both = jnp.concatenate([block, (rows == cols).astype(jnp.float32)], axis=1)
    groups = [both[8 * n : 8 * n + 8, :] for n in range(size // 8)]
    pivots = []
    for own in range(size // 8):
        live = range(own, size // 8)
        spread = [
            {n: jnp.broadcast_to(groups[n][:, 8 * own + i : 8 * own + i + 1], (8, width)) for n in live} for i in range(8)
        ]
        for i in range(8):
            column = spread[i]
            pivot = column[own][i : i + 1, :]
            pivots.append(pivot[:, :1])
            inverse = 1.0 / pivot
            below = dict(column)
            below[own] = jnp.where(sub > i, column[own], 0.0)
            for later in range(i + 1, 8):
                factor = column[own][later : later + 1, :] * inverse
                for n in live:
                    spread[later][n] = spread[later][n] - below[n] * factor
            scaled = groups[own][i : i + 1, :] * inverse
            for n in live:
                groups[n] = groups[n] - below[n] * scaled
    done = jnp.concatenate(groups, axis=0)
    return done[:, size:] * (1.0 / jnp.sqrt(jnp.concatenate(pivots, axis=0)))


def eliminate(work, starts):
    rank, size = work.shape[0], 64
    for start in starts:
        here = slice(start, start + size)
        strip = dot_f32(lower_inverse(work[here, here]), work[here, :], ((1,), (0,)), highest)
        work[here, :] = strip
        if start + size < rank:
            work[start + size :, :] -= dot_f32(strip[:, start + size : rank], strip, ((0,), (0,)), highest)


def gram_kernel(own_ref, other_ref, mixed_ref, work):
    rows, rank = own_ref.shape[0], mixed_ref.shape[1]
    p = jnp.concatenate([own_ref[:, :rank], other_ref[:, :rank]], axis=0)
    m_own = dot_f32(own_ref[:, rank:], p, ((1,), (0,)), highest)
    m_other = dot_f32(other_ref[:, rank + rows :], p[:rows], ((1,), (0,)), highest)
    m_other += dot_f32(other_ref[:, rank : rank + rows], p[rows:], ((1,), (0,)), highest)
    m = jnp.concatenate([m_own, m_other], axis=0)
    mixed_ref[...] = m
    work[:, :rank] = dot_f32(p, m, ((0,), (0,)), highest)
    row_ids = lax.broadcasted_iota(jnp.int32, (rank, rank), 0)
    col_ids = lax.broadcasted_iota(jnp.int32, (rank, rank), 1)
    work[:, rank:] = (row_ids == col_ids).astype(jnp.float32)
    eliminate(work, (0, 64))


def dion_gram(own, other, rank):
    return pl.pallas_call(
        gram_kernel,
        out_shape=[
            jax.ShapeDtypeStruct((2 * own.shape[0], rank), jnp.float32),
            jax.ShapeDtypeStruct((rank, 2 * rank), jnp.float32),
        ],
        compiler_params=pltpu.CompilerParams(vmem_limit_bytes=40 << 20),
        cost_estimate=pl.CostEstimate(flops=5 << 30, bytes_accessed=4 << 20, transcendentals=0),
        name="dion_gram",
    )(own, other)


def mixes_kernel(own_ref, other_ref, mixed_ref, half_ref, left_ref, right_ref, work):
    rows, rank = own_ref.shape[0], mixed_ref.shape[1]
    work[...] = half_ref[...]
    eliminate(work, (128, 192))
    inverse = work[:, rank:]
    left_ref[:rows, :] = dot_f32(own_ref[:, :rank], inverse, ((1,), (1,)), highest) * math.sqrt(D)
    left_ref[rows:, :] = dot_f32(other_ref[:, :rank], inverse, ((1,), (1,)), highest) * math.sqrt(D)
    right_ref[...] = dot_f32(mixed_ref[...], inverse, ((1,), (1,)), highest)


def dion_mixes(own, other, mixed, half):
    return pl.pallas_call(
        mixes_kernel,
        out_shape=[jax.ShapeDtypeStruct(mixed.shape, jnp.float32)] * 2,
        scratch_shapes=[pltpu.VMEM(half.shape, jnp.float32)],
        compiler_params=pltpu.CompilerParams(vmem_limit_bytes=40 << 20),
        cost_estimate=pl.CostEstimate(flops=5 << 30, bytes_accessed=4 << 20, transcendentals=0),
        name="dion_mixes",
    )(own, other, mixed, half)


def factors_kernel(info, left_mix, right_mix, x_ref, x_other_ref, g_ref, left_ref, right_ref):
    rows = x_ref.shape[0]
    left_ref[0] = times_exact(x_ref[...], left_mix[:rows, :]) + times_exact(x_other_ref[...], left_mix[rows:, :])
    right_ref[0] = times_exact(g_ref[...], right_mix[...])


def dion_factors(info, left_mix, right_mix, inputs, inputs_other, query_grad):
    tokens, width = query_grad.shape
    rank = left_mix.shape[1]
    mix = pl.BlockSpec((tokens, rank), lambda i, info: (0, 0))
    columns = pl.BlockSpec((tokens // 2, width), lambda i, info: (0, info[1]))
    result = pl.BlockSpec((1, width, rank), lambda i, info: (0, 0, 0))
    return pl.pallas_call(
        factors_kernel,
        out_shape=[jax.ShapeDtypeStruct((1, width, rank), jnp.float32)] * 2,
        grid_spec=pltpu.PrefetchScalarGridSpec(
            num_scalar_prefetch=1,
            grid=(1,),
            in_specs=[mix, mix, columns, columns, pl.BlockSpec((tokens, width), lambda i, info: (0, 0))],
            out_specs=[result, result],
        ),
        compiler_params=pltpu.CompilerParams(vmem_limit_bytes=40 << 20),
        cost_estimate=pl.CostEstimate(flops=2 << 30, bytes_accessed=4 << 20, transcendentals=0),
        name="dion_factors",
    )(info, left_mix, right_mix, inputs, inputs_other, query_grad)


def after(value, other):
    return lax.optimization_barrier((value, other))[0]


def swap_cores(value):
    return lax.ppermute(value, "tensor", [(i, i ^ 1) for i in range(2 * ZN)])


def along_z(value, steps):
    count = 2 * ZN
    return lax.ppermute(value, "tensor", [(i, (i + 2 * steps) % count) for i in range(count)])


def exchange_z(value):
    return lax.all_to_all(value, "tensor", 0, 0, tiled=True, axis_index_groups=z_groups)


def shift_sections(value, core_flip):
    sections, count = lax.axis_size("section"), lax.axis_size("tensor")
    pairs = [(s * count + t, (s - 1) * count + (t ^ core_flip)) for s in range(1, sections) for t in range(count)]
    return lax.ppermute(value, ("section", "tensor"), pairs)


def local(queries, key_rows, value_rows, out_grad, layer_input, query_weight, dion_basis, lengths):
    tokens, width = queries.shape[1:]
    tensor_index = lax.axis_index("tensor")
    z, core = tensor_index // 2, tensor_index % 2
    group_head = tensor_index * (width // HD) // GROUP
    info = jnp.stack([z, core, group_head]).astype(jnp.int32)
    half_tokens = tokens // 2

    w_other = swap_cores(query_weight)
    basis_other = swap_cores(dion_basis)

    by_column = layer_input[0].reshape(CHUNK, ZN, D // ZN).transpose(1, 0, 2)
    own_columns = exchange_z(by_column).reshape(half_tokens, D // ZN)

    query_grad = attention(info, lengths, queries, out_grad, key_rows, value_rows)
    grad_other = swap_cores(query_grad)

    up, down, rest = layer_partial(info, query_grad, grad_other, query_weight, w_other)

    own_columns = after(own_columns, up)
    other_columns = swap_cores(own_columns)
    chip_part = chip_parts(query_grad, grad_other, dion_basis, basis_other, own_columns, other_columns)
    summands = exchange_z(chip_part.reshape(ZN, CHUNK, chip_part.shape[1]))
    rows = 2 * CHUNK
    up_rest = [rest[rows * n : rows * (n + 1)] for n in range(3)]
    down_rest = [rest[rows * (3 + n) : rows * (4 + n)] for n in range(3)]

    own = jnp.sum(summands, axis=0)
    own = jnp.broadcast_to(own[None], (ZN,) + own.shape)
    gathered = exchange_z(own).reshape(half_tokens, own.shape[2])
    gathered_other = swap_cores(gathered)
    for n in range(3):
        up, down = along_z(up, 1), along_z(down, -1)
        if n == 1:
            up, down = after((up, down), own)
        if n == 2:
            up, down = after((up, down), gathered)
        up, down = up + up_rest[n], down + down_rest[n]
    half = up.shape[1] // 2
    last_up, last_down = along_z(up[:, :half], 1), along_z(down[:, half:], -1)

    mixed, eliminated = dion_gram(gathered, gathered_other, dion_basis.shape[2])

    def total(a, b):
        return (a.astype(jnp.float32) + b.astype(jnp.float32)).astype(jnp.bfloat16)

    last_up, last_down = after((last_up, last_down), eliminated)
    summed = jnp.concatenate([total(last_up, down[:, :half]), total(last_down, up[:, half:])], axis=1)

    from_own = shift_sections(summed[:CHUNK], 0)
    from_other = shift_sections(summed[CHUNK:], 1)
    left_mix, right_mix = dion_mixes(gathered, gathered_other, after(mixed, summed), eliminated)
    left_factor, right_factor = dion_factors(info, left_mix, right_mix, own_columns, other_columns, query_grad)
    from_own, from_other = after((from_own, from_other), left_factor)
    upstream = jnp.where(
        core == 0,
        jnp.concatenate([from_own, from_other], axis=1),
        jnp.concatenate([from_other, from_own], axis=1),
    )
    return (upstream[None], left_factor, right_factor)


def solution(mesh):
    placed = (
        P("section", None, "tensor"),
        P("section", None, None),
        P("section", None, None),
        P("section", None, "tensor"),
        P("section", "tensor", None),
        P("section", None, "tensor"),
        P("section", "tensor", None),
        P("section", None),
    )
    return jax.shard_map(
        local,
        mesh=mesh,
        in_specs=placed,
        out_specs=(
            P("section", "tensor", None),
            P("section", "tensor", None),
            P("section", "tensor", None),
        ),
        check_vma=False,
    )
```

```python
import functools
import math

import jax
import jax.numpy as jnp
from jax import lax
from jax.experimental import pallas as pl
from jax.experimental.pallas import tpu as pltpu
from jax.sharding import PartitionSpec as P

D = 8192
HD = 128
GROUP = 8
ZN = 8
CHUNK = 32

rope_base = 500000.0
highest = lax.Precision.HIGHEST
z_groups = [[2 * z + core for z in range(ZN)] for core in range(2)]


def dot_f32(a, b, dims, precision=None):
    return lax.dot_general(a, b, (dims, ((), ())), precision=precision, preferred_element_type=jnp.float32)


def attention_kernel(info, lens, q_ref, g_ref, k_ref, v_ref, out_ref, bias, cos_ref, sin_ref):
    block = 256
    tokens, width = q_ref.shape[1:]
    core = info[1]
    scale = 1.0 / math.sqrt(HD)

    @pl.when(pl.program_id(0) == 0)
    def _():
        bound_one = lens[0, 0]
        bound_two = lens[0, 0] + lens[0, 1]
        i = lax.broadcasted_iota(jnp.int32, bias.shape, 0)
        j = lax.broadcasted_iota(jnp.int32, bias.shape, 1)
        crossed = (i >= bound_two) & (j >= bound_one) & (j < bound_two)
        visible = (j <= i) & jnp.logical_not(crossed)
        bias[...] = jnp.where(visible, 0.0, -jnp.inf)
        token = lax.broadcasted_iota(jnp.int32, cos_ref.shape, 0)
        position = jnp.where(token < bound_two, token, token - lens[0, 1]).astype(jnp.float32)
        lane = lax.broadcasted_iota(jnp.int32, cos_ref.shape, 1)
        freq_ids = jnp.where(lane < HD // 2, lane, lane - HD // 2).astype(jnp.float32)
        angle = position * jnp.exp(-math.log(rope_base) * 2.0 * freq_ids / HD)
        cos_ref[...] = jnp.cos(angle)
        sin_ref[...] = jnp.where(lane < HD // 2, 1.0, -1.0) * jnp.sin(angle)

    for row in range(0, tokens, block):
        keys = row + block
        here = slice(row, row + block)
        k = k_ref[0, :keys, :]
        v = v_ref[0, :keys, :]
        for head in range(0, width, HD):
            lanes = slice(head, head + HD)
            s = dot_f32(q_ref[0, here, lanes], k, ((1,), (1,))) + bias[here, :keys]
            dp = dot_f32(g_ref[0, here, lanes], v, ((1,), (1,)))
            e = jnp.exp2((s - jnp.max(s, axis=-1, keepdims=True)) * (scale * math.log2(math.e)))
            w = e * (1.0 / jnp.sum(e, axis=-1, keepdims=True))
            low = w.astype(jnp.bfloat16).astype(jnp.float32)
            out_dot = jnp.sum(low * dp, axis=-1, keepdims=True)
            ds = (w * (dp - out_dot)).astype(jnp.bfloat16)
            r = dot_f32(ds, k, ((1,), (0,))) * scale
            turned = jnp.concatenate([r[:, HD // 2 :], r[:, : HD // 2]], axis=1)
            r = (r * cos_ref[here, :] + turned * sin_ref[here, :]).astype(jnp.bfloat16)
            for n in range(block // CHUNK):
                chip, side = divmod(row // CHUNK + n, 2)
                target = pl.multiple_of((core ^ side) * (tokens // 2) + chip * CHUNK, CHUNK)
                out_ref[pl.ds(target, CHUNK), lanes] = r[n * CHUNK : (n + 1) * CHUNK, :]


def attention(info, lengths, queries, out_grad, key_rows, value_rows):
    tokens, width = queries.shape[1:]
    heads = width // HD
    pair = 2 * HD
    head_block = pl.BlockSpec((1, tokens, pair), lambda h, info, lens: (0, 0, h))
    kv_block = pl.BlockSpec((1, tokens, HD), lambda h, info, lens: (0, 0, info[2]))
    return pl.pallas_call(
        attention_kernel,
        out_shape=jax.ShapeDtypeStruct((tokens, width), jnp.bfloat16),
        grid_spec=pltpu.PrefetchScalarGridSpec(
            num_scalar_prefetch=2,
            grid=(width // pair,),
            in_specs=[head_block, head_block, kv_block, kv_block],
            out_specs=pl.BlockSpec((tokens, pair), lambda h, info, lens: (0, h)),
            scratch_shapes=[pltpu.VMEM((tokens, tokens), jnp.float32)] + [pltpu.VMEM((tokens, HD), jnp.float32)] * 2,
        ),
        compiler_params=pltpu.CompilerParams(vmem_limit_bytes=58 << 20),
        cost_estimate=pl.CostEstimate(flops=1 << 20, bytes_accessed=1 << 20, transcendentals=0),
        name="attention_backward",
    )(info, lengths, queries, out_grad, key_rows, value_rows)


up_cars = ((4, 3, 2, 1), (3, 2, 1, 0))
down_cars = ((5, 6, 7, 0), (4, 5, 6, 7))


def layer_kernel(info, mine_ref, other_ref, w_mine_ref, w_other_ref, up_ref, down_ref, rest_ref, rows_a, rows_b):
    z = info[0]
    step, steps = pl.program_id(0), pl.num_programs(0)
    cars = up_ref.shape[0]

    @pl.when(step == 0)
    def _():
        for half in range(2):
            for place, chip in enumerate((up_cars[half][0], down_cars[half][0]) + up_cars[half][1:] + down_cars[half][1:]):
                start = lax.rem(z + chip, ZN) * CHUNK
                for side in range(2):
                    target = slice((2 * place + side) * CHUNK, (2 * place + side + 1) * CHUNK)
                    rows_a[half, target, :] = mine_ref[pl.ds(pl.multiple_of(start + side * ZN * CHUNK, CHUNK), CHUNK), :]
                    start_b = pl.multiple_of(start + (1 - side) * ZN * CHUNK, CHUNK)
                    rows_b[half, target, :] = other_ref[pl.ds(start_b, CHUNK), :]

    half = lax.div(2 * step, steps)
    total = dot_f32(rows_a[half], w_mine_ref[0], ((1,), (1,)))
    total += dot_f32(rows_b[half], w_other_ref[0], ((1,), (1,)))
    total = total.astype(jnp.bfloat16)
    up_ref[...] = total[:cars]
    down_ref[...] = total[cars : 2 * cars]
    rest_ref[...] = total[2 * cars :]


def layer_partial(info, mine, other, w_mine, w_other):
    tokens, width = mine.shape
    columns = w_other.shape[1] // 2
    tile = 1024
    steps = columns // tile
    rows = [2 * CHUNK, 2 * CHUNK, tokens - 4 * CHUNK]
    whole = pl.BlockSpec((tokens, width), lambda i, info: (0, 0))
    weight = pl.BlockSpec((1, tile, width), lambda i, info: (0, info[1] * steps + i, 0))
    return pl.pallas_call(
        layer_kernel,
        out_shape=[jax.ShapeDtypeStruct((count, columns), jnp.bfloat16) for count in rows],
        grid_spec=pltpu.PrefetchScalarGridSpec(
            num_scalar_prefetch=1,
            grid=(steps,),
            in_specs=[whole, whole, weight, weight],
            out_specs=[pl.BlockSpec((count, tile), lambda i, info: (0, i)) for count in rows],
            scratch_shapes=[pltpu.VMEM((2, tokens, width), jnp.bfloat16)] * 2,
        ),
        compiler_params=pltpu.CompilerParams(vmem_limit_bytes=56 << 20),
        cost_estimate=pl.CostEstimate(flops=1 << 20, bytes_accessed=1 << 20, transcendentals=0),
        name="layer_partial",
    )(info, mine, other, w_mine, w_other)


def split_three(value):
    high = value.astype(jnp.bfloat16)
    rest = value - high.astype(jnp.float32)
    middle = rest.astype(jnp.bfloat16)
    low = (rest - middle.astype(jnp.float32)).astype(jnp.bfloat16)
    return high, middle, low


def times_exact(narrow, wide):
    parts = [dot_f32(narrow, part, ((0,), (0,))) for part in split_three(wide)]
    return parts[0] + (parts[1] + parts[2])


def parts_kernel(mine_ref, other_ref, basis_ref, basis_other_ref, x_ref, x_other_ref, out_ref):
    rows, rank = mine_ref.shape[0], basis_ref.shape[2]
    total = None
    for grad, basis in ((mine_ref, basis_ref), (other_ref, basis_other_ref)):
        for piece in split_three(basis[0]):
            term = dot_f32(grad[...], piece, ((1,), (0,)))
            total = term if total is None else total + term
    out_ref[:, :rank] = total
    out_ref[:, rank : rank + rows] = dot_f32(x_ref[...], x_ref[...], ((1,), (1,)))
    out_ref[:, rank + rows :] = dot_f32(x_ref[...], x_other_ref[...], ((1,), (1,)))


def chip_parts(mine, other, basis, basis_other, inputs, inputs_other):
    rows = inputs.shape[0]
    width, rank = basis.shape[1:]
    upper = pl.BlockSpec((rows, width), lambda i: (0, 0))
    lower = pl.BlockSpec((rows, width), lambda i: (1, 0))
    whole = [pl.BlockSpec(value.shape, lambda i, n=value.ndim: (0,) * n) for value in (basis, basis_other, inputs, inputs_other)]
    return pl.pallas_call(
        parts_kernel,
        out_shape=jax.ShapeDtypeStruct((rows, rank + 2 * rows), jnp.float32),
        grid=(1,),
        in_specs=[upper, lower] + whole,
        out_specs=pl.BlockSpec((rows, rank + 2 * rows), lambda i: (0, 0)),
        compiler_params=pltpu.CompilerParams(vmem_limit_bytes=40 << 20),
        cost_estimate=pl.CostEstimate(flops=1 << 30, bytes_accessed=4 << 20, transcendentals=0),
        name="chip_parts",
    )(mine, other, basis, basis_other, inputs, inputs_other)


def lower_inverse(block):
    size = block.shape[0]
    width = 2 * size
    rows = lax.broadcasted_iota(jnp.int32, (size, size), 0)
    cols = lax.broadcasted_iota(jnp.int32, (size, size), 1)
    sub = lax.broadcasted_iota(jnp.int32, (8, width), 0)
    both = jnp.concatenate([block, (rows == cols).astype(jnp.float32)], axis=1)
    groups = [both[8 * n : 8 * n + 8, :] for n in range(size // 8)]
    pivots = []
    for own in range(size // 8):
        live = range(own, size // 8)
        spread = [
            {n: jnp.broadcast_to(groups[n][:, 8 * own + i : 8 * own + i + 1], (8, width)) for n in live} for i in range(8)
        ]
        for i in range(8):
            column = spread[i]
            pivot = column[own][i : i + 1, :]
            pivots.append(pivot[:, :1])
            inverse = 1.0 / pivot
            below = dict(column)
            below[own] = jnp.where(sub > i, column[own], 0.0)
            for later in range(i + 1, 8):
                factor = column[own][later : later + 1, :] * inverse
                for n in live:
                    spread[later][n] = spread[later][n] - below[n] * factor
            scaled = groups[own][i : i + 1, :] * inverse
            for n in live:
                groups[n] = groups[n] - below[n] * scaled
    done = jnp.concatenate(groups, axis=0)
    return done[:, size:] * (1.0 / jnp.sqrt(jnp.concatenate(pivots, axis=0)))


def eliminate(work, starts):
    rank, size = work.shape[0], 64
    for start in starts:
        here = slice(start, start + size)
        strip = dot_f32(lower_inverse(work[here, here]), work[here, :], ((1,), (0,)), highest)
        work[here, :] = strip
        if start + size < rank:
            work[start + size :, :] -= dot_f32(strip[:, start + size : rank], strip, ((0,), (0,)), highest)


def gram_kernel(own_ref, other_ref, mixed_ref, work):
    rows, rank = own_ref.shape[0], mixed_ref.shape[1]
    p = jnp.concatenate([own_ref[:, :rank], other_ref[:, :rank]], axis=0)
    m_own = dot_f32(own_ref[:, rank:], p, ((1,), (0,)), highest)
    m_other = dot_f32(other_ref[:, rank + rows :], p[:rows], ((1,), (0,)), highest)
    m_other += dot_f32(other_ref[:, rank : rank + rows], p[rows:], ((1,), (0,)), highest)
    m = jnp.concatenate([m_own, m_other], axis=0)
    mixed_ref[...] = m
    work[:, :rank] = dot_f32(p, m, ((0,), (0,)), highest)
    row_ids = lax.broadcasted_iota(jnp.int32, (rank, rank), 0)
    col_ids = lax.broadcasted_iota(jnp.int32, (rank, rank), 1)
    work[:, rank:] = (row_ids == col_ids).astype(jnp.float32)
    eliminate(work, (0, 64))


def dion_gram(own, other, rank):
    return pl.pallas_call(
        gram_kernel,
        out_shape=[
            jax.ShapeDtypeStruct((2 * own.shape[0], rank), jnp.float32),
            jax.ShapeDtypeStruct((rank, 2 * rank), jnp.float32),
        ],
        compiler_params=pltpu.CompilerParams(vmem_limit_bytes=40 << 20),
        cost_estimate=pl.CostEstimate(flops=5 << 30, bytes_accessed=4 << 20, transcendentals=0),
        name="dion_gram",
    )(own, other)


def mixes_kernel(own_ref, other_ref, mixed_ref, half_ref, left_ref, right_ref, work):
    rows, rank = own_ref.shape[0], mixed_ref.shape[1]
    work[...] = half_ref[...]
    eliminate(work, (128, 192))
    inverse = work[:, rank:]
    left_ref[:rows, :] = dot_f32(own_ref[:, :rank], inverse, ((1,), (1,)), highest) * math.sqrt(D)
    left_ref[rows:, :] = dot_f32(other_ref[:, :rank], inverse, ((1,), (1,)), highest) * math.sqrt(D)
    right_ref[...] = dot_f32(mixed_ref[...], inverse, ((1,), (1,)), highest)


def dion_mixes(own, other, mixed, half):
    return pl.pallas_call(
        mixes_kernel,
        out_shape=[jax.ShapeDtypeStruct(mixed.shape, jnp.float32)] * 2,
        scratch_shapes=[pltpu.VMEM(half.shape, jnp.float32)],
        compiler_params=pltpu.CompilerParams(vmem_limit_bytes=40 << 20),
        cost_estimate=pl.CostEstimate(flops=5 << 30, bytes_accessed=4 << 20, transcendentals=0),
        name="dion_mixes",
    )(own, other, mixed, half)


def factors_kernel(info, left_mix, right_mix, x_ref, x_other_ref, g_ref, left_ref, right_ref):
    rows = x_ref.shape[0]
    left_ref[0] = times_exact(x_ref[...], left_mix[:rows, :]) + times_exact(x_other_ref[...], left_mix[rows:, :])
    right_ref[0] = times_exact(g_ref[...], right_mix[...])


def dion_factors(info, left_mix, right_mix, inputs, inputs_other, query_grad):
    tokens, width = query_grad.shape
    rank = left_mix.shape[1]
    mix = pl.BlockSpec((tokens, rank), lambda i, info: (0, 0))
    columns = pl.BlockSpec((tokens // 2, width), lambda i, info: (0, info[1]))
    result = pl.BlockSpec((1, width, rank), lambda i, info: (0, 0, 0))
    return pl.pallas_call(
        factors_kernel,
        out_shape=[jax.ShapeDtypeStruct((1, width, rank), jnp.float32)] * 2,
        grid_spec=pltpu.PrefetchScalarGridSpec(
            num_scalar_prefetch=1,
            grid=(1,),
            in_specs=[mix, mix, columns, columns, pl.BlockSpec((tokens, width), lambda i, info: (0, 0))],
            out_specs=[result, result],
        ),
        compiler_params=pltpu.CompilerParams(vmem_limit_bytes=40 << 20),
        cost_estimate=pl.CostEstimate(flops=2 << 30, bytes_accessed=4 << 20, transcendentals=0),
        name="dion_factors",
    )(info, left_mix, right_mix, inputs, inputs_other, query_grad)


def column_kernel(rows_ref, out_ref):
    width = out_ref.shape[2]
    for n in range(out_ref.shape[0]):
        out_ref[n] = rows_ref[0, :, n * width : (n + 1) * width]


def column_blocks(rows):
    return pl.pallas_call(
        column_kernel,
        out_shape=jax.ShapeDtypeStruct((ZN, rows.shape[1], rows.shape[2] // ZN), rows.dtype),
        compiler_params=pltpu.CompilerParams(vmem_limit_bytes=58 << 20),
        cost_estimate=pl.CostEstimate(flops=0, bytes_accessed=1 << 20, transcendentals=0),
        name="column_blocks",
    )(rows)


def after(value, other):
    return lax.optimization_barrier((value, other))[0]


def swap_cores(value):
    return lax.ppermute(value, "tensor", [(i, i ^ 1) for i in range(2 * ZN)])


def along_z(value, steps):
    count = 2 * ZN
    return lax.ppermute(value, "tensor", [(i, (i + 2 * steps) % count) for i in range(count)])


def exchange_z(value):
    return lax.all_to_all(value, "tensor", 0, 0, tiled=True, axis_index_groups=z_groups)


def shift_sections(value, core_flip):
    sections, count = lax.axis_size("section"), lax.axis_size("tensor")
    pairs = [(s * count + t, (s - 1) * count + (t ^ core_flip)) for s in range(1, sections) for t in range(count)]
    return lax.ppermute(value, ("section", "tensor"), pairs)


def local(queries, key_rows, value_rows, out_grad, layer_input, query_weight, dion_basis, lengths):
    tokens, width = queries.shape[1:]
    tensor_index = lax.axis_index("tensor")
    z, core = tensor_index // 2, tensor_index % 2
    group_head = tensor_index * (width // HD) // GROUP
    info = jnp.stack([z, core, group_head]).astype(jnp.int32)
    half_tokens = tokens // 2

    w_other = swap_cores(query_weight)
    basis_other = swap_cores(dion_basis)

    by_column = column_blocks(layer_input)
    own_columns = exchange_z(by_column).reshape(half_tokens, D // ZN)

    query_grad = attention(info, lengths, queries, out_grad, key_rows, value_rows)
    grad_other = swap_cores(query_grad)

    up, down, rest = layer_partial(info, query_grad, grad_other, query_weight, w_other)

    own_columns = after(own_columns, up)
    other_columns = swap_cores(own_columns)
    chip_part = chip_parts(query_grad, grad_other, dion_basis, basis_other, own_columns, other_columns)
    summands = exchange_z(chip_part.reshape(ZN, CHUNK, chip_part.shape[1]))
    rows = 2 * CHUNK
    up_rest = [rest[rows * n : rows * (n + 1)] for n in range(3)]
    down_rest = [rest[rows * (3 + n) : rows * (4 + n)] for n in range(3)]

    own = jnp.sum(summands, axis=0)
    own = jnp.broadcast_to(own[None], (ZN,) + own.shape)
    gathered = exchange_z(own).reshape(half_tokens, own.shape[2])
    gathered_other = swap_cores(gathered)
    for n in range(3):
        up, down = along_z(up, 1), along_z(down, -1)
        if n == 1:
            up, down = after((up, down), own)
        if n == 2:
            up, down = after((up, down), gathered)
        up, down = up + up_rest[n], down + down_rest[n]
    half = up.shape[1] // 2
    last_up, last_down = along_z(up[:, :half], 1), along_z(down[:, half:], -1)

    mixed, eliminated = dion_gram(gathered, gathered_other, dion_basis.shape[2])

    def total(a, b):
        return (a.astype(jnp.float32) + b.astype(jnp.float32)).astype(jnp.bfloat16)

    last_up, last_down = after((last_up, last_down), eliminated)
    summed = jnp.concatenate([total(last_up, down[:, :half]), total(last_down, up[:, half:])], axis=1)

    from_own = shift_sections(summed[:CHUNK], 0)
    from_other = shift_sections(summed[CHUNK:], 1)
    left_mix, right_mix = dion_mixes(gathered, gathered_other, after(mixed, summed), eliminated)
    left_factor, right_factor = dion_factors(info, left_mix, right_mix, own_columns, other_columns, query_grad)
    from_own, from_other = after((from_own, from_other), left_factor)
    upstream = jnp.where(
        core == 0,
        jnp.concatenate([from_own, from_other], axis=1),
        jnp.concatenate([from_other, from_own], axis=1),
    )
    return (upstream[None], left_factor, right_factor)


def solution(mesh):
    placed = (
        P("section", None, "tensor"),
        P("section", None, None),
        P("section", None, None),
        P("section", None, "tensor"),
        P("section", "tensor", None),
        P("section", None, "tensor"),
        P("section", "tensor", None),
        P("section", None),
    )
    return jax.shard_map(
        local,
        mesh=mesh,
        in_specs=placed,
        out_specs=(
            P("section", "tensor", None),
            P("section", "tensor", None),
            P("section", "tensor", None),
        ),
        check_vma=False,
    )
```
